32 devices in a mesh: group: 2 (over x), wide: 16 (over z, y, core).
Axes of the slice: x: 2, y: 2, z: 4, core: 2. Of those that a mesh axis runs over, the one named last changes fastest.
Arguments:
- visibilities: float32 [6144, 2, 128], P(('group', 'wide')), parts along dimension 0, may hold values from -6 to 6
- offsets: float32 [6144, 2, 128], P(('group', 'wide')), parts along dimension 0, may hold values from 2 to 30
- vis_count: int32 [6144], P(('group', 'wide')), parts along dimension 0, may hold values from 1 to 128, 294912 in all
- owner: int32 [6144], P(('group', 'wide')), parts along dimension 0, may hold values from 0 to 15, as said below
- tile_row: int32 [6144], P(('group', 'wide')), parts along dimension 0, may hold values from 0 to 7
- tile_col: int32 [6144], P(('group', 'wide')), parts along dimension 0, may hold values from 0 to 127
Outputs:
- image: float32 [2, 8192, 4096], P(None, 'group', 'wide'), parts along dimension 1
The draws below stay inside these ranges and needn't reach their ends.
There are 2 independent parts, one for each index of `group`. The reference program is written for one: setup_inputs(seed, part) draws one part's arguments, and reference() takes and returns one part's arrays. A program takes and returns all parts, laid end to end along the dimension named above; each array names one. Nothing has to cross between parts.
Inputs may be any that keep to these rules, and one draw needn't show every extreme that they name: At most 36 subgrids of one device have the same owner; in every draw one owner receives exactly 36 subgrids from every device. `vis_count`: the live visibilities of a subgrid are the first ones of its slots; some subgrid has all 128 live; over each part along group the counts sum to 294912.
All inputs are finite; a program needn't handle non-finite values.
Results may differ from the reference program's by a relative error of at most 0.0003.
Values sent between devices are 32-bit elements; how exact they have to be, the bound alone decides.
A program may use at most 128 MiB of HBM per device.

```python
import math
import jax
import jax.numpy as jnp
import numpy as np
from jax import lax

SUB = 32
VIS = 128
SUB_DEV = 192
GRID = 4096
OWNERS = 16
SUBGRIDS = 3072
CAP = 36
TROWS = 8
TCOLS = 128


def draw_owner(key, part):
    hot_key, bias_key, row_key = jax.random.split(key, 3)
    hottest = jax.random.randint(hot_key, (), 0, OWNERS)
    owner_bias = jax.random.randint(bias_key, (OWNERS,), 0, 4 * CAP)
    slot_index = jnp.arange(OWNERS * CAP).reshape(OWNERS, CAP)
    is_hot = jnp.arange(OWNERS)[:, None] == hottest
    rest_count = SUB_DEV - CAP

    def one_device(device_key):
        noise_key, order_key = jax.random.split(device_key)
        noise_draw = jax.random.randint(noise_key, (OWNERS, CAP), 0, 2 * CAP)
        scores = (owner_bias[:, None] + noise_draw) * (OWNERS * CAP) + slot_index
        scores = jnp.where(is_hot, -1, scores)
        chosen = lax.top_k(scores.reshape(-1), rest_count)[1] // CAP
        targets = jnp.concatenate([jnp.full((CAP,), hottest, jnp.int32), chosen.astype(jnp.int32)])
        return targets[jax.random.permutation(order_key, SUB_DEV)]
    device_keys = jax.random.split(row_key, OWNERS)
    return jax.vmap(one_device)(device_keys).reshape(-1).astype(jnp.int32)


def touch_ends(array, own_key, low, top_value):
    extent = array.shape
    spot = [jax.random.randint(jax.random.fold_in(own_key, axis), (), 0, extent[axis]) for axis in range(len(extent))]
    array = array.at[tuple(spot)].set(low)
    longest = extent.index(max(extent))
    spot[longest] = (spot[longest] + 1) % extent[longest]
    return array.at[tuple(spot)].set(top_value)


def block_scale(rng, extent, cuts, low, largest):
    def one(dim, blocks):
        steps = jax.random.uniform(jax.random.fold_in(jax.random.fold_in(rng, 6), dim), (blocks,), jnp.float32, low / len(cuts), largest / len(cuts))
        return jnp.repeat(jnp.exp(steps), extent[dim] // blocks).reshape((-1,) + (1,) * (len(extent) - dim - 1))

    level = one(*cuts[0])
    for cut in cuts[1:]:
        level = level * one(*cut)
    return level


def rank_table(amount, slope):
    weights = [(1 << 20) // math.isqrt(rank ** slope) + 1 for rank in range(1, amount + 1)]
    deviation = 1 + sum(weights) // (1 << 30)
    return np.cumsum(np.array([max(1, weight // deviation) for weight in weights]))


def ranked_ids(own_key, shape, amount, lean):
    grid = rank_table(amount, lean)
    lot = jax.random.randint(jax.random.fold_in(own_key, 1), shape, 0, int(grid[amount - 1]))
    standing = jnp.searchsorted(jnp.asarray(grid, jnp.int32), lot, side="right")
    return jax.random.permutation(jax.random.fold_in(own_key, 2), amount)[standing].astype(jnp.int32)


def length_profile(number_of, total, most, skew):
    portions = [(1 << 20) // math.isqrt(standing ** skew) + 1 for standing in range(2, number_of + 1)]
    rest, holding = total - most - (number_of - 1), [1] * (number_of - 1)
    while rest > 0:
        candidates = [i for i in range(number_of - 1) if holding[i] < most]
        pool, budget = sum([portions[i] for i in candidates]), rest
        for i in candidates:
            more = min(most - holding[i], max(1, budget * portions[i] // pool), rest)
            holding[i] = holding[i] + more
            rest = rest - more
    return np.array([most] + holding)


def uneven(key, amount, total, reach, slope):
    if amount == 2:
        one = jax.random.randint(key, (), max(1, total - reach), min(reach, total - 1) + 1)
        return jnp.stack([one, total - one])
    sizes = jnp.asarray(length_profile(amount, total, reach, slope), jnp.int32)
    pairs = (amount - 1) // 2
    source_of, receiver = sizes[1:1 + 2 * pairs:2], sizes[2:2 + 2 * pairs:2]
    room = jnp.minimum(source_of - 1, reach - receiver)
    moved = jax.random.randint(jax.random.fold_in(key, 1), (pairs,), 0, 1 << 20) % (room + 1)
    sizes = sizes.at[1:1 + 2 * pairs:2].set(source_of - moved).at[2:2 + 2 * pairs:2].set(receiver + moved)
    return sizes[jax.random.permutation(jax.random.fold_in(key, 2), amount)]


def normal_values(rng, dims, scale, reach, pieces=(), kind=jnp.bfloat16):
    values = jax.random.normal(rng, dims, jnp.float32) * scale
    if len(pieces) > 0:
        values = block_scale(rng, dims, pieces, -0.22, 0.18) * values
    return jnp.clip(values, min=-reach, max=reach).astype(kind)


def setup_inputs(seed: int = 0, part: int = 0) -> dict:
    key_list = jax.random.split(jax.random.key(seed), 7)
    part_keys = jax.random.split(jax.random.fold_in(key_list[6], part), 7)
    return {
        "visibilities": normal_values(part_keys[0], (SUBGRIDS, 2, VIS), 1.0, 6.0, ((0, 16),), jnp.float32),
        "offsets": jnp.clip(2.0 + 28.0 * jax.random.uniform(part_keys[1], (SUBGRIDS, 2, VIS), jnp.float32) ** block_scale(part_keys[1], (SUBGRIDS, 2, VIS), ((0, 16),), -0.2, 0.2), 2.0, 30.0),
        "vis_count": uneven(part_keys[2], SUBGRIDS, 3 * SUBGRIDS * VIS // 4, VIS, 1).astype(jnp.int32),
        "owner": draw_owner(jax.random.fold_in(jax.random.fold_in(key_list[6], part), 71), part),
        "tile_row": touch_ends(jax.random.randint(part_keys[4], (SUBGRIDS,), 0, TROWS), jax.random.fold_in(part_keys[4], 1), 0, TROWS - 1).astype(jnp.int32),
        "tile_col": touch_ends(ranked_ids(part_keys[5], (SUBGRIDS,), TCOLS, 2), jax.random.fold_in(part_keys[5], 3), 0, TCOLS - 1).astype(jnp.int32),
    }


highest = lax.Precision.HIGHEST

def cplx_einsum(pattern, left_real, left_imag, right_real, right_imag):

    def single(first, second):
        return jnp.einsum(pattern, first, second, precision=highest)
    return (single(left_real, right_real) - single(left_imag, right_imag), single(left_real, right_imag) + single(left_imag, right_real))

def subgrid_pixels(samples, counts):
    position = (jnp.arange(SUB, dtype=jnp.float32) - SUB // 2) / SUB
    live_mask = jnp.where(jnp.arange(VIS)[None, :] < counts[:, None], 1.0 / math.sqrt(VIS), 0.0)
    vis_real = samples[:, 0] * live_mask
    vis_imag = samples[:, 1] * live_mask
    angle_u = 2.0 * math.pi * samples[:, 2, :, None] * position
    angle_v = 2.0 * math.pi * samples[:, 3, :, None] * position
    cos_u, sin_u = (jnp.cos(angle_u), jnp.sin(angle_u))
    cos_v, sin_v = (jnp.cos(angle_v), jnp.sin(angle_v))
    weight_real = vis_real[:, :, None] * cos_u - vis_imag[:, :, None] * sin_u
    weight_imag = vis_real[:, :, None] * sin_u + vis_imag[:, :, None] * cos_u
    return cplx_einsum('nki,nkj->nij', weight_real, weight_imag, cos_v, sin_v)

def reference(visibilities, offsets, vis_count, owner, tile_row, tile_col):
    samples = jnp.concatenate([visibilities, offsets], axis=1).reshape(OWNERS, SUB_DEV, 4, VIS)
    counts = vis_count.reshape(OWNERS, SUB_DEV)

    def block_spectra(block_args):
        block_samples, block_counts = block_args
        pixel_real, pixel_imag = subgrid_pixels(block_samples, block_counts)
        spectra = jnp.fft.fft2(pixel_real + 1j * pixel_imag, norm='ortho')
        return jnp.stack([jnp.real(spectra), jnp.imag(spectra)], axis=1)
    spectra = lax.map(block_spectra, (samples, counts)).reshape(SUBGRIDS, 2, SUB, SUB)
    tile_index = (owner * TROWS + tile_row) * TCOLS + tile_col
    grid_tiles = jnp.zeros((GRID // SUB * TCOLS, 2, SUB, SUB), spectra.dtype).at[tile_index].add(spectra)
    grid_full = grid_tiles.reshape(GRID // SUB, TCOLS, 2, SUB, SUB).transpose(2, 0, 3, 1, 4).reshape(2, GRID, GRID)
    image = jnp.fft.fft2(grid_full[0] + 1j * grid_full[1], norm='ortho')
    return jnp.stack([jnp.real(image), jnp.imag(image)]).astype(jnp.float32)
```

```python
import functools
import math

import jax
import jax.numpy as jnp
import numpy as np
from jax import lax
from jax.experimental import pallas as pl
from jax.experimental.pallas import tpu as pltpu
from jax.sharding import PartitionSpec as P

SUB = 32
HALF = SUB // 2
VIS = 128
GRID = 4096
TILES = GRID // SUB
F32 = jnp.float32
BF16 = jnp.bfloat16


def _poly_coefs():
    nodes = 0.125 * (1 + np.cos(np.pi * (np.arange(64) + 0.5) / 64))
    r = np.sqrt(nodes)
    cheb = np.polynomial.chebyshev.Chebyshev
    c = cheb.fit(nodes, np.cos(2 * np.pi * r), 5, domain=[0, 0.25])
    s = cheb.fit(nodes, np.sin(2 * np.pi * r) / r, 5, domain=[0, 0.25])
    poly = np.polynomial.Polynomial
    return (
        [float(v) for v in c.convert(kind=poly).coef],
        [float(v) for v in s.convert(kind=poly).coef],
    )


COS_C, SIN_C = _poly_coefs()


def cis(turns):
    r = turns - jnp.round(turns)
    z = r * r
    c = COS_C[5]
    s = SIN_C[5]
    for k in range(4, -1, -1):
        c = c * z + COS_C[k]
        s = s * z + SIN_C[k]
    return c, s * r


def split(x):
    hi = x.astype(BF16)
    lo = (x - hi.astype(F32)).astype(BF16)
    return hi, lo


def np_tables():
    t = np.arange(SUB)
    q = np.arange(SUB)
    n0 = np.arange(TILES)
    g = np.einsum(
        "tq,qn->tn",
        np.exp(-2j * np.pi * np.outer(t, q) / SUB),
        np.exp(-2j * np.pi * np.outer(q, n0) / GRID),
    )
    w = np.exp(-2j * np.pi * (np.outer(n0, n0) % TILES) / TILES)
    return g, w


def to_waves(g):
    up = g[:, HALF:]
    down = g[:, HALF - 1 :: -1]
    return np.concatenate([up + down, 1j * (up - down)], 1)


def shifted(g):
    index = (np.arange(SUB)[:, None] + np.arange(SUB)[None, :]) % SUB
    return to_waves(g[index])


def pixel_rows(raw_ref, size, out_ref, row_ref):
    step = (lax.broadcasted_iota(jnp.int32, (8, VIS), 0).astype(F32) + 0.5) / SUB
    lane = lax.broadcasted_iota(jnp.int32, (16, VIS), 1)
    cat = jnp.concatenate

    def prepare(t):
        ar, ai, u, v = (raw_ref[q * size + t * 8 : q * size + t * 8 + 8] for q in range(4))
        pr, pi = cis((u + v) * (-1.0 / (2 * SUB)))
        ur, ui = cis(u * 0.25)
        vr, vi = cis(v * 0.25)
        rows = [u, v, ur, ui, vr, vi, ar * pr - ai * pi, ar * pi + ai * pr]
        for q, row in enumerate(rows):
            row_ref[t, q] = row

    def wave(turns, r8, i8):
        c0, s0 = cis(turns * step)
        return [c0, c0 * r8 - s0 * i8, s0, c0 * i8 + s0 * r8]

    def one(t, d):
        bc = lambda q: jnp.broadcast_to(row_ref[t, q, d : d + 1, :], (8, VIS))
        u, v, ur, ui, vr, vi, ar, ai = (bc(q) for q in range(8))
        us = cat(wave(u, ur, ui), 0)
        vs = wave(v, vr, vi)
        bs = cat([ar * x for x in vs] + [ai * x for x in vs], 0)
        uh, ul = split(us)
        bh, bl = split(bs)
        prod = lax.dot_general(
            cat([uh, ul], 1),
            cat([cat([bh, bh], 1), cat([bl, bl], 1)], 0),
            (((1,), (1,)), ((), ())),
            preferred_element_type=F32,
        )
        q = prod + pltpu.roll(prod, 64, 1)
        out_ref[t * 8 + d] = jnp.where(lane < 64, q[:16], q[16:])

    for t in range(size // 8):
        prepare(t)
    for t in range(size // 8):
        for d in range(8):
            one(t, d)


def gather_kernel(
    wide, subs, size, lag, count_ref, vis_ref, off_ref, tile_ref, pix_hbm, ids_hbm,
    raw_ref, row_ref, out_ref,
    send_sem, recv_sem, loc_sem, pix_send, pix_recv, id_loc, id_send, id_recv,
):
    depth = wide // 4
    pieces = subs // size
    trips = 2 * depth * pieces
    me = lax.axis_index("wide")
    core, y, z = me % 2, (me // 2) % 2, me // 4
    place = lambda zz, yy, cc: (zz * 2 + yy) * 2 + cc
    partner = {"wide": place(z, y, 1 - core)}
    across = {"wide": place(z, 1 - y, core)}
    above = {"wide": place(jnp.minimum(z + 1, depth - 1), y, core)}
    below = {"wide": place(jnp.maximum(z - 1, 0), y, core)}
    not_top, not_bottom = z < depth - 1, z > 0
    mesh_id = pl.DeviceIdType.MESH
    here = z * 2 + y

    barrier = pltpu.get_barrier_semaphore()
    for peer in (partner, across):
        pl.semaphore_signal(barrier, inc=1, device_id=peer, device_id_type=mesh_id)

    @pl.when(not_top)
    def _():
        pl.semaphore_signal(barrier, inc=1, device_id=above, device_id_type=mesh_id)

    @pl.when(not_bottom)
    def _():
        pl.semaphore_signal(barrier, inc=1, device_id=below, device_id_type=mesh_id)

    slots = lax.broadcasted_iota(jnp.int32, (2, VIS), 1)

    def stage(t, carry):
        piece = t * 8 // size
        base = t * 8 - piece * size
        for d in range(8):
            n = t * 8 + d
            live = jnp.where(slots < count_ref[n], 1.0 / math.sqrt(VIS), 0.0)
            for half, pair in enumerate((vis_ref[n] * live, off_ref[n])):
                for q in range(2):
                    row = (half * 2 + q) * size + base + d
                    raw_ref[here, piece, pl.ds(row, 1), :] = pair[q : q + 1]
        return carry

    lax.fori_loop(0, subs // 8, stage, 0)
    for piece in range(pieces):
        raw_ref[here, piece, 4 * size :, :] = tile_ref[piece]
    neighbours = jnp.minimum(z, 1) + jnp.minimum(depth - 1 - z, 1)
    pl.semaphore_wait(barrier, 2 + neighbours)

    def hop(zz, yy, piece, to, way):
        chip = zz * 2 + yy
        return pltpu.make_async_remote_copy(
            src_ref=raw_ref.at[chip, piece],
            dst_ref=raw_ref.at[chip, piece],
            send_sem=send_sem.at[zz, piece, way],
            recv_sem=recv_sem.at[chip, piece],
            device_id=to,
            device_id_type=mesh_id,
        )

    def spread_out(zz, piece, act):
        act(hop(zz, y, piece, across, 2))

        @pl.when((zz <= z) & not_top)
        def _():
            act(hop(zz, y, piece, above, 0))

        @pl.when((zz >= z) & not_bottom)
        def _():
            act(hop(zz, y, piece, below, 1))

    for piece in range(pieces):
        spread_out(z, piece, lambda copy: copy.start())

    def pass_on(number):
        far, piece = number // pieces + 1, number % pieces
        for zz, inside in ((z - far, z - far >= 0), (z + far, z + far < depth)):

            @pl.when(inside)
            def _():
                hop(zz, y, piece, across, 2).wait_recv()
                spread_out(zz, piece, lambda copy: copy.start())

    def order(k):
        near = jnp.minimum(z, depth - 1 - z)
        swing = z + ((k + 1) // 2) * (1 - 2 * (k % 2))
        edge = jnp.where(z * 2 < depth - 1, k, depth - 1 - k)
        return jnp.where(k <= 2 * near, swing, edge)

    def copies(number, chip, piece):
        rows = pl.ds((chip * 2 + core) * subs + piece * size, size)
        slot = number % 2
        mine = pltpu.make_async_copy(out_ref.at[slot], pix_hbm.at[rows], loc_sem.at[slot])
        theirs = pltpu.make_async_remote_copy(
            src_ref=out_ref.at[slot],
            dst_ref=pix_hbm.at[rows],
            send_sem=pix_send.at[slot],
            recv_sem=pix_recv.at[number],
            device_id=partner,
            device_id_type=mesh_id,
        )
        return mine, theirs

    def id_copies(number, chip, piece):
        block = raw_ref.at[chip, piece, pl.ds(4 * size, 8)]
        where = ids_hbm.at[(chip * 2 + core) * pieces + piece]
        mine = pltpu.make_async_copy(block, where, id_loc.at[number])
        theirs = pltpu.make_async_remote_copy(
            src_ref=block,
            dst_ref=where,
            send_sem=id_send.at[number],
            recv_sem=id_recv.at[number],
            device_id=partner,
            device_id_type=mesh_id,
        )
        return mine, theirs

    def body(number, carry):
        s, piece = number // pieces, number % pieces
        zz = order(s // 2)
        yy = y + (s % 2) * (1 - 2 * y)
        chip = zz * 2 + yy

        @pl.when(s % 2 == 1)
        def _():
            hop(zz, yy, piece, across, 2).wait_recv()

        for copy in id_copies(number, chip, piece):
            copy.start()

        @pl.when(number >= 2)
        def _():
            mine, theirs = copies(number, chip, piece)
            mine.wait()
            theirs.wait_send()

        pixel_rows(raw_ref.at[chip, piece], size, out_ref.at[number % 2], row_ref)
        for copy in copies(number, chip, piece):
            copy.start()

        @pl.when((number >= lag) & (number < lag + (depth - 1) * pieces))
        def _():
            pass_on(number - lag)

        return carry

    lax.fori_loop(0, trips, body, 0)

    def drain(number, carry):
        spread_out(number // pieces, number % pieces, lambda copy: copy.wait_send())
        return carry

    lax.fori_loop(0, depth * pieces, drain, 0)
    for number in range(2):
        mine, theirs = copies(number, here, 0)
        mine.wait()
        theirs.wait_send()

    def arrive(number, carry):
        mine, theirs = id_copies(number, here, 0)
        mine.wait()
        theirs.wait()
        copies(number, here, 0)[1].wait_recv()
        return carry

    lax.fori_loop(0, trips, arrive, 0)


def gather(counts, visibilities, offsets, tile, wide, size):
    subs = visibilities.shape[0]
    depth = wide // 4
    pieces = subs // size
    trips = 2 * depth * pieces
    dma = pltpu.SemaphoreType.DMA
    anywhere = pl.BlockSpec(memory_space=pl.ANY)
    whole = pl.BlockSpec(memory_space=pltpu.VMEM)
    return pl.pallas_call(
        functools.partial(gather_kernel, wide, subs, size, min(4, 2 * pieces - 1)),
        out_shape=[
            jax.ShapeDtypeStruct((wide * subs, 16, 128), F32),
            jax.ShapeDtypeStruct((wide * pieces, 8, 128), F32),
        ],
        in_specs=[pl.BlockSpec(memory_space=pltpu.SMEM), whole, whole, whole],
        out_specs=[anywhere, anywhere],
        scratch_shapes=[
            pltpu.VMEM((wide // 2, pieces, 4 * size + 8, 128), F32),
            pltpu.VMEM((size // 8, 8, 8, VIS), F32),
            pltpu.VMEM((2, size, 16, 128), F32),
            dma((depth, pieces, 3)),
            dma((wide // 2, pieces)),
            dma((2,)),
            dma((2,)),
            dma((trips,)),
            dma((trips,)),
            dma((trips,)),
            dma((trips,)),
        ],
        compiler_params=pltpu.CompilerParams(collective_id=0, has_side_effects=True),
        name="gather",
    )(counts, visibilities, offsets, tile)


def fft(xs):
    n = len(xs)
    if n == 1:
        return xs
    even, odd = fft(xs[::2]), fft(xs[1::2])
    low, high = [], []
    root = math.sqrt(0.5)
    for k, ((er, ei), (r, i)) in enumerate(zip(even, odd)):
        if k == 0:
            tr, ti = r, i
        elif 4 * k == n:
            low.append((er + i, ei - r))
            high.append((er - i, ei + r))
            continue
        elif 8 * k == n:
            tr, ti = (r + i) * root, (i - r) * root
        elif 8 * k == 3 * n:
            tr, ti = (i - r) * root, (r + i) * -root
        else:
            tr, ti = turn(r, i, k / n)
        low.append((er + tr, ei + ti))
        high.append((er - tr, ei - ti))
    return low + high


def turn(r, i, turns):
    c, s = math.cos(2 * math.pi * turns), math.sin(2 * math.pi * turns)
    return r * c + i * s, i * c - r * s


def finish_kernel(
    block, nc, shift, p_ref, ids_ref, phr_ref, phi_ref, waves_hbm, mix_hbm, out_hbm,
    x_ref, b_ref, y_ref, tab_ref, wave_ref, mix_ref, idv_ref, ids_smem, sem, id_sem, mix_sem,
):
    g = pl.program_id(0)
    steps = pl.num_programs(0)
    halves = nc // 128
    chunk = 16
    rows = chunk * 16

    @pl.when(g == 0)
    def _():
        first = lax.axis_index("wide") * halves
        pltpu.make_async_copy(mix_hbm, mix_ref, mix_sem).start()
        load = pltpu.make_async_copy(waves_hbm.at[pl.ds(first, halves)], wave_ref, sem)
        load.start()

        def number(t, carry):
            idv_ref[pl.ds(t, 1), :] = ids_ref[t, 0:1, :].astype(jnp.int32)
            return carry

        lax.fori_loop(0, ids_ref.shape[0], number, 0, unroll=4)
        scalars = pltpu.make_async_copy(idv_ref, ids_smem, id_sem)
        scalars.start()

        def zero(t, carry):
            for lt in range(2 * halves):
                for ref in (b_ref, x_ref):
                    ref[lt, pl.ds(t * 32, 32), :] = jnp.zeros((32, 128), F32)
            return carry

        lax.fori_loop(0, TILES, zero, 0)
        load.wait()
        tab_ref[192:256] = jnp.zeros((64, 2 * nc), BF16)
        for n in range(halves):
            left = slice(n * 128, n * 128 + 128)
            right = slice(nc + n * 128, nc + n * 128 + 128)
            for part in range(3):
                dr = wave_ref[n, part // 2 * 64 : part // 2 * 64 + 32]
                di = wave_ref[n, part // 2 * 64 + 32 : part // 2 * 64 + 64]
                tab_ref[part * 64 : part * 64 + 32, left] = dr
                tab_ref[part * 64 + 32 : part * 64 + 64, left] = -di
                tab_ref[part * 64 : part * 64 + 32, right] = di
                tab_ref[part * 64 + 32 : part * 64 + 64, right] = dr
        scalars.wait()

    lane = lax.broadcasted_iota(jnp.int32, (rows, 128), 1)

    def multiply(t, slot):
        p = p_ref[pl.ds(t * chunk, chunk)].reshape(rows, 128)
        hi = p.astype(BF16)
        hif = hi.astype(F32)
        lof = p - hif
        hir = pltpu.roll(hif, 64, 1)
        lor = pltpu.roll(lof, 64, 1)
        one = jnp.where(lane < 64, hif, lor).astype(BF16)
        two = jnp.where(lane < 64, hir, lof).astype(BF16)
        lhs = jnp.concatenate(
            [
                jnp.concatenate([one, hi], 1),
                jnp.concatenate([two, hir.astype(BF16)], 1),
            ],
            0,
        )
        y_ref[slot] = jnp.dot(lhs, tab_ref[...], preferred_element_type=F32)

    def add(t, slot):
        for d in range(chunk):
            tile = ids_smem[g, t * chunk + d]
            r = lax.shift_right_logical(tile, shift)
            c = lax.bitwise_and(tile, TILES - 1)
            pr = jnp.broadcast_to(phr_ref[pl.ds(c, 1), :], (8, 128))
            pi = jnp.broadcast_to(phi_ref[pl.ds(c, 1), :], (8, 128))
            dst = pl.ds(pl.multiple_of(r * 32, 32), 32)
            acc = b_ref if d % 2 else x_ref
            old = acc[:, dst, :]
            tops = y_ref[slot, pl.ds(d * 16, 16), :]
            bots = y_ref[slot, pl.ds(rows + d * 16, 16), :]
            y = jnp.concatenate([tops, bots], 0)
            real, imag = [], []
            for n in range(halves):
                yr = y[:, n * 128 : n * 128 + 128].reshape(4, 8, 128)
                yi = y[:, nc + n * 128 : nc + n * 128 + 128].reshape(4, 8, 128)
                real.append((yr * pr - yi * pi).reshape(1, 32, 128))
                imag.append((yr * pi + yi * pr).reshape(1, 32, 128))
            acc[:, dst, :] = old + jnp.concatenate(real + imag, 0)

    trips = block // chunk
    multiply(0, 0)
    for t in range(trips):
        if t + 1 < trips:
            multiply(t + 1, (t + 1) % 2)
        add(t, t % 2)

    @pl.when(g == steps - 1)
    def _():
        at = lambda r, it: pl.ds(pl.multiple_of(r * 32 + it * 8, 8), 8)

        def eights(t, carry):
            n, it = t // 4, t % 4
            for b in range(16):
                xs = []
                for a in range(8):
                    pick = at(16 * a + b, it)
                    xs.append(
                        tuple(
                            x_ref[o * halves + n, pick, :] + b_ref[o * halves + n, pick, :]
                            for o in range(2)
                        )
                    )
                for k, (r, i) in enumerate(fft(xs)):
                    if b * k:
                        r, i = turn(r, i, b * k / TILES)
                    pick = at(16 * k + b, it)
                    x_ref[n, pick, :] = r
                    x_ref[halves + n, pick, :] = i
            return carry

        def sixteens(t, carry):
            n, it = t // 4, t % 4
            for a in range(8):
                xs = []
                for b in range(16):
                    pick = at(16 * a + b, it)
                    xs.append((x_ref[n, pick, :], x_ref[halves + n, pick, :]))
                for k, (r, i) in enumerate(fft(xs)):
                    pick = at(a + 8 * k, it)
                    b_ref[n, pick, :] = r
                    b_ref[halves + n, pick, :] = i
            return carry

        lax.fori_loop(0, 4 * halves, eights, 0)
        lax.fori_loop(0, 4 * halves, sixteens, 0)
        pltpu.make_async_copy(mix_hbm, mix_ref, mix_sem).wait()

        def mix(m, carry):
            near = pl.ds(pl.multiple_of(m * SUB, SUB), SUB)
            far = pl.ds(m, SUB, stride=TILES)
            zm = jnp.concatenate(
                [
                    jnp.concatenate([b_ref[o * halves + n, near, :] for n in range(halves)], 1)
                    for o in range(2)
                ],
                0,
            )
            zh, zl = split(zm)
            both = mix_ref[m]
            res = jnp.dot(
                jnp.concatenate([both, both[:, :64]], 1),
                jnp.concatenate([zh, zh, zl], 0),
                preferred_element_type=F32,
            )
            for p in range(2):
                for n in range(halves):
                    x_ref[p * halves + n, far, :] = res[
                        p * 32 : p * 32 + 32, n * 128 : n * 128 + 128
                    ]
            return carry

        lax.fori_loop(0, TILES, mix, 0, unroll=8)
        stores = [
            pltpu.make_async_copy(
                x_ref.at[p * halves + n],
                out_hbm.at[p, :, pl.ds(n * 128, 128)],
                sem,
            )
            for p in range(2)
            for n in range(halves)
        ]
        for store in stores:
            store.start()
        for store in stores:
            store.wait()


def finish(pix, ids, phr, phi, waves, mix, nc, block):
    count = pix.shape[0]
    tiles = 2 * nc // 128
    const = lambda shape: pl.BlockSpec(shape, lambda g: (0,) * len(shape))
    anywhere = pl.BlockSpec(memory_space=pl.ANY)
    x_shape = (tiles, GRID, 128)
    dma = pltpu.SemaphoreType.DMA
    return pl.pallas_call(
        functools.partial(finish_kernel, block, nc, TILES.bit_length() - 1),
        out_shape=jax.ShapeDtypeStruct((2, GRID, nc), F32),
        grid=(count // block,),
        in_specs=[
            pl.BlockSpec((block, 16, 128), lambda g: (g, 0, 0)),
            const(ids.shape),
            const(phr.shape),
            const(phi.shape),
            anywhere,
            anywhere,
        ],
        out_specs=anywhere,
        scratch_shapes=[
            pltpu.VMEM(x_shape, F32),
            pltpu.VMEM(x_shape, F32),
            pltpu.VMEM((2, 512, 2 * nc), F32),
            pltpu.VMEM((256, 2 * nc), BF16),
            pltpu.VMEM((nc // 128, 128, 128), BF16),
            pltpu.VMEM(mix.shape, BF16),
            pltpu.VMEM((count // block, 128), jnp.int32),
            pltpu.SMEM((count // block, 128), jnp.int32),
            dma,
            dma,
            dma,
        ],
        name="finish",
    )(pix, ids, phr, phi, waves, mix)


def np_split(x):
    hi = x.astype(np.float32).astype(BF16)
    return hi, (x - hi.astype(np.float64)).astype(BF16)


def column_waves(g):
    waves = shifted(g) / 512.0
    rh, rl = np_split(waves.real)
    ih, il = np_split(waves.imag)
    return np.concatenate([rh, ih, rl, il], 1)


def real_form(z):
    return np.array([[z.real, -z.imag], [z.imag, z.real]])


def per_device(visibilities, offsets, vis_count, owner, tile_row, tile_col):
    wide = lax.axis_size("wide")
    nc = GRID // wide
    band = GRID // (SUB * wide)
    g, w = np_tables()
    subs = visibilities.shape[0]
    size = math.gcd(subs, 64)
    tile = ((owner * band + tile_row) * TILES + tile_col).astype(F32)
    tile = jnp.pad(tile.reshape(subs // size, 1, size), ((0, 0), (0, 7), (0, 128 - size)))
    pix, ids = gather(vis_count, visibilities, offsets, tile, wide, size)
    m4 = real_form(shifted(g) / 256.0).transpose(4, 0, 2, 1, 3).reshape(TILES, 64, 64)
    both = jnp.asarray(np.concatenate(np_split(m4), 2))
    phr, phi = jnp.asarray(w.real, F32), jnp.asarray(w.imag, F32)
    return finish(pix, ids, phr, phi, jnp.asarray(column_waves(g)), both, nc, size)


def solution(mesh):
    placed = (
        P(("group", "wide"), None, None),
        P(("group", "wide"), None, None),
        P(("group", "wide")),
        P(("group", "wide")),
        P(("group", "wide")),
        P(("group", "wide")),
    )
    return jax.shard_map(
        per_device, mesh=mesh, in_specs=placed, out_specs=P(None, "group", "wide"), check_vma=False
    )
```

```python
import functools
import math

import jax
import jax.numpy as jnp
import numpy as np
from jax import lax
from jax.experimental import pallas as pl
from jax.experimental.pallas import tpu as pltpu
from jax.sharding import PartitionSpec as P

SUB = 32
HALF = SUB // 2
VIS = 128
GRID = 4096
TILES = GRID // SUB
F32 = jnp.float32
BF16 = jnp.bfloat16


def _poly_coefs():
    top = ((SUB - 4) / 2 / (2 * SUB)) ** 2
    nodes = top / 2 * (1 + np.cos(np.pi * (np.arange(64) + 0.5) / 64))
    r = np.sqrt(nodes)
    cheb = np.polynomial.chebyshev.Chebyshev
    c = cheb.fit(nodes, np.cos(2 * np.pi * r), 4, domain=[0, top])
    s = cheb.fit(nodes, np.sin(2 * np.pi * r) / r, 4, domain=[0, top])
    poly = np.polynomial.Polynomial
    return (
        [float(v) for v in c.convert(kind=poly).coef],
        [float(v) for v in s.convert(kind=poly).coef],
    )


COS_C, SIN_C = _poly_coefs()


def cis(r):
    z = r * r
    c = COS_C[4]
    s = SIN_C[4]
    for k in range(3, -1, -1):
        c = c * z + COS_C[k]
        s = s * z + SIN_C[k]
    return c, s * r


def cmul(a, b):
    return a[0] * b[0] - a[1] * b[1], a[0] * b[1] + a[1] * b[0]


def split(x):
    hi = x.astype(BF16)
    lo = (x - hi.astype(F32)).astype(BF16)
    return hi, lo


def np_tables():
    t = np.arange(SUB)
    q = np.arange(SUB)
    n0 = np.arange(TILES)
    g = np.einsum(
        "tq,qn->tn",
        np.exp(-2j * np.pi * np.outer(t, q) / SUB),
        np.exp(-2j * np.pi * np.outer(q, n0) / GRID),
    )
    w = np.exp(-2j * np.pi * (np.outer(n0, n0) % TILES) / TILES)
    return g, w


def to_waves(g):
    sign = (-1.0) ** np.arange(HALF)[None, :, None]
    up = g[:, HALF:] * sign
    down = g[:, HALF - 1 :: -1] * -sign
    return np.concatenate([up + down, 1j * (up - down)], 1)


def shifted(g):
    index = (np.arange(SUB)[:, None] + np.arange(SUB)[None, :]) % SUB
    return to_waves(g[index])


def pixel_rows(raw_ref, size, out_ref, row_ref, wave_ref):
    lane = lax.broadcasted_iota(jnp.int32, (SUB, VIS), 1)
    cat = jnp.concatenate

    def prepare(t):
        ar, ai, u, v = (raw_ref[q * size + t * 8 : q * size + t * 8 + 8] for q in range(4))
        firsts, steps = [], []
        for axis, offset in enumerate((u, v)):
            base = cis((offset - HALF) * (1.0 / (2 * SUB)))
            twice = cmul(base, base)
            wave = base
            for m in range(8):
                if m:
                    wave = cmul(wave, twice)
                for part in range(2):
                    row = t * 8 * SUB + (axis * 2 + part) * 8 + m
                    wave_ref[pl.ds(row, 8, stride=SUB), :] = wave[part]
            firsts.append(base)
            steps.append(cmul(wave, base))
        pr, pi = cmul(*firsts)
        rows = [*steps[0], *steps[1], ar * pr + ai * pi, ai * pr - ar * pi]
        for q, row in enumerate(rows):
            row_ref[t, q] = row

    def parts(n):
        t, d = n // 8, n % 8
        bc = lambda q: jnp.broadcast_to(row_ref[t, q, d : d + 1, :], (8, VIS))
        ur, ui, vr, vi, ar, ai = (bc(q) for q in range(6))
        cu, su, cv, sv = (wave_ref[n * SUB + q * 8 : n * SUB + q * 8 + 8] for q in range(4))
        ahead = lambda c, s, r, i: [c, c * r - s * i, s, c * i + s * r]
        us = ahead(cu, su, ur, ui)
        vs = ahead(cv, sv, vr, vi)
        bs = [ar * x for x in vs] + [ai * x for x in vs]
        uh, ul = split(cat(us, 0))
        bh, bl = split(cat(bs, 0))
        return cat([uh, ul, uh], 1), cat([bh, bh, bl], 1)

    def pair(n):
        one, two = parts(n), parts(n + 1)
        prod = lax.dot_general(
            cat([one[0], two[0]], 0),
            cat([one[1], two[1]], 0),
            (((1,), (1,)), ((), ())),
            preferred_element_type=F32,
        )
        out_ref[n // 2] = jnp.where(lane < 64, prod[:SUB], prod[SUB:])

    prepare(0)
    for t in range(size // 8):
        if t + 1 < size // 8:
            prepare(t + 1)
        for d in range(0, 8, 2):
            pair(t * 8 + d)


def gather_kernel(
    wide, subs, size, lag, count_ref, vis_ref, off_ref, tile_ref, pix_hbm, ids_hbm,
    raw_ref, row_ref, wave_ref, out_ref,
    send_sem, recv_sem, loc_sem, pix_send, pix_recv, id_loc, id_send, id_recv,
):
    depth = wide // 4
    pieces = subs // size
    trips = 2 * depth * pieces
    me = lax.axis_index("wide")
    core, y, z = me % 2, (me // 2) % 2, me // 4
    place = lambda zz, yy, cc: (zz * 2 + yy) * 2 + cc
    partner = {"wide": place(z, y, 1 - core)}
    across = {"wide": place(z, 1 - y, core)}
    above = {"wide": place(jnp.minimum(z + 1, depth - 1), y, core)}
    below = {"wide": place(jnp.maximum(z - 1, 0), y, core)}
    not_top, not_bottom = z < depth - 1, z > 0
    mesh_id = pl.DeviceIdType.MESH
    here = z * 2 + y

    barrier = pltpu.get_barrier_semaphore()
    for peer in (partner, across):
        pl.semaphore_signal(barrier, inc=1, device_id=peer, device_id_type=mesh_id)

    @pl.when(not_top)
    def _():
        pl.semaphore_signal(barrier, inc=1, device_id=above, device_id_type=mesh_id)

    @pl.when(not_bottom)
    def _():
        pl.semaphore_signal(barrier, inc=1, device_id=below, device_id_type=mesh_id)

    slots = lax.broadcasted_iota(jnp.int32, (2, VIS), 1)

    def stage(t, carry):
        piece = t * 8 // size
        base = t * 8 - piece * size
        for d in range(8):
            n = t * 8 + d
            live = jnp.where(slots < count_ref[n], 1.0 / math.sqrt(VIS), 0.0)
            for half, pair in enumerate((vis_ref[n] * live, off_ref[n])):
                for q in range(2):
                    row = (half * 2 + q) * size + base + d
                    raw_ref[here, piece, pl.ds(row, 1), :] = pair[q : q + 1]
        return carry

    lax.fori_loop(0, subs // 8, stage, 0)
    for piece in range(pieces):
        raw_ref[here, piece, 4 * size :, :] = tile_ref[piece]
    neighbours = jnp.minimum(z, 1) + jnp.minimum(depth - 1 - z, 1)
    pl.semaphore_wait(barrier, 2 + neighbours)

    def hop(zz, yy, piece, to, way):
        chip = zz * 2 + yy
        return pltpu.make_async_remote_copy(
            src_ref=raw_ref.at[chip, piece],
            dst_ref=raw_ref.at[chip, piece],
            send_sem=send_sem.at[zz, piece, way],
            recv_sem=recv_sem.at[chip, piece],
            device_id=to,
            device_id_type=mesh_id,
        )

    def spread_out(zz, piece, act):
        act(hop(zz, y, piece, across, 2))

        @pl.when((zz <= z) & not_top)
        def _():
            act(hop(zz, y, piece, above, 0))

        @pl.when((zz >= z) & not_bottom)
        def _():
            act(hop(zz, y, piece, below, 1))

    for piece in range(pieces):
        spread_out(z, piece, lambda copy: copy.start())

    def pass_on(number):
        far, piece = number // pieces + 1, number % pieces
        for zz, inside in ((z - far, z - far >= 0), (z + far, z + far < depth)):

            @pl.when(inside)
            def _():
                hop(zz, y, piece, across, 2).wait_recv()
                spread_out(zz, piece, lambda copy: copy.start())

    def order(k):
        near = jnp.minimum(z, depth - 1 - z)
        swing = z + ((k + 1) // 2) * (1 - 2 * (k % 2))
        edge = jnp.where(z * 2 < depth - 1, k, depth - 1 - k)
        return jnp.where(k <= 2 * near, swing, edge)

    def copies(number, chip, piece):
        rows = pl.ds(((chip * 2 + core) * subs + piece * size) // 2, size // 2)
        slot = number % 2
        mine = pltpu.make_async_copy(out_ref.at[slot], pix_hbm.at[rows], loc_sem.at[slot])
        theirs = pltpu.make_async_remote_copy(
            src_ref=out_ref.at[slot],
            dst_ref=pix_hbm.at[rows],
            send_sem=pix_send.at[slot],
            recv_sem=pix_recv.at[number],
            device_id=partner,
            device_id_type=mesh_id,
        )
        return mine, theirs

    def id_copies(number, chip, piece):
        block = raw_ref.at[chip, piece, pl.ds(4 * size, 8)]
        where = ids_hbm.at[(chip * 2 + core) * pieces + piece]
        mine = pltpu.make_async_copy(block, where, id_loc.at[number])
        theirs = pltpu.make_async_remote_copy(
            src_ref=block,
            dst_ref=where,
            send_sem=id_send.at[number],
            recv_sem=id_recv.at[number],
            device_id=partner,
            device_id_type=mesh_id,
        )
        return mine, theirs

    def body(number, carry):
        s, piece = number // pieces, number % pieces
        zz = order(s // 2)
        yy = y + (s % 2) * (1 - 2 * y)
        chip = zz * 2 + yy

        @pl.when(s % 2 == 1)
        def _():
            hop(zz, yy, piece, across, 2).wait_recv()

        for copy in id_copies(number, chip, piece):
            copy.start()

        @pl.when(number >= 2)
        def _():
            mine, theirs = copies(number, chip, piece)
            mine.wait()
            theirs.wait_send()

        pixel_rows(raw_ref.at[chip, piece], size, out_ref.at[number % 2], row_ref, wave_ref)
        for copy in copies(number, chip, piece):
            copy.start()

        @pl.when((number >= lag) & (number < lag + (depth - 1) * pieces))
        def _():
            pass_on(number - lag)

        return carry

    lax.fori_loop(0, trips, body, 0)

    def drain(number, carry):
        spread_out(number // pieces, number % pieces, lambda copy: copy.wait_send())
        return carry

    lax.fori_loop(0, depth * pieces, drain, 0)
    for number in range(2):
        mine, theirs = copies(number, here, 0)
        mine.wait()
        theirs.wait_send()

    def arrive(number, carry):
        mine, theirs = id_copies(number, here, 0)
        mine.wait()
        theirs.wait()
        copies(number, here, 0)[1].wait_recv()
        return carry

    lax.fori_loop(0, trips, arrive, 0)


def gather(counts, visibilities, offsets, tile, wide, size):
    subs = visibilities.shape[0]
    depth = wide // 4
    pieces = subs // size
    trips = 2 * depth * pieces
    dma = pltpu.SemaphoreType.DMA
    anywhere = pl.BlockSpec(memory_space=pl.ANY)
    whole = pl.BlockSpec(memory_space=pltpu.VMEM)
    return pl.pallas_call(
        functools.partial(gather_kernel, wide, subs, size, min(4, 2 * pieces - 1)),
        out_shape=[
            jax.ShapeDtypeStruct((wide * subs // 2, SUB, 128), F32),
            jax.ShapeDtypeStruct((wide * pieces, 8, 128), F32),
        ],
        in_specs=[pl.BlockSpec(memory_space=pltpu.SMEM), whole, whole, whole],
        out_specs=[anywhere, anywhere],
        scratch_shapes=[
            pltpu.VMEM((wide // 2, pieces, 4 * size + 8, 128), F32),
            pltpu.VMEM((size // 8, 6, 8, VIS), F32),
            pltpu.VMEM((size * SUB, VIS), F32),
            pltpu.VMEM((2, size // 2, SUB, 128), F32),
            dma((depth, pieces, 3)),
            dma((wide // 2, pieces)),
            dma((2,)),
            dma((2,)),
            dma((trips,)),
            dma((trips,)),
            dma((trips,)),
            dma((trips,)),
        ],
        compiler_params=pltpu.CompilerParams(collective_id=0, has_side_effects=True),
        name="gather",
    )(counts, visibilities, offsets, tile)


def fft(xs):
    n = len(xs)
    if n == 1:
        return xs
    even, odd = fft(xs[::2]), fft(xs[1::2])
    low, high = [], []
    root = math.sqrt(0.5)
    for k, ((er, ei), (r, i)) in enumerate(zip(even, odd)):
        if k == 0:
            tr, ti = r, i
        elif 4 * k == n:
            low.append((er + i, ei - r))
            high.append((er - i, ei + r))
            continue
        elif 8 * k == n:
            tr, ti = (r + i) * root, (i - r) * root
        elif 8 * k == 3 * n:
            tr, ti = (i - r) * root, (r + i) * -root
        else:
            tr, ti = turn(r, i, k / n)
        low.append((er + tr, ei + ti))
        high.append((er - tr, ei - ti))
    return low + high


def turn(r, i, turns):
    c, s = math.cos(2 * math.pi * turns), math.sin(2 * math.pi * turns)
    return r * c + i * s, i * c - r * s


def finish_kernel(
    block, nc, shift, p_ref, ids_ref, phr_ref, phi_ref, waves_hbm, mix_hbm, out_hbm,
    x_ref, b_ref, y_ref, tab_ref, wave_ref, mix_ref, idv_ref, ids_smem, sem, id_sem, mix_sem, out_sem,
):
    g = pl.program_id(0)
    steps = pl.num_programs(0)
    halves = nc // 128
    chunk = 16
    rows = chunk * 16

    @pl.when(g == 0)
    def _():
        first = lax.axis_index("wide") * halves
        pltpu.make_async_copy(mix_hbm, mix_ref, mix_sem).start()
        load = pltpu.make_async_copy(waves_hbm.at[pl.ds(first, halves)], wave_ref, sem)
        load.start()

        def number(t, carry):
            idv_ref[pl.ds(t, 1), :] = ids_ref[t, 0:1, :].astype(jnp.int32)
            return carry

        lax.fori_loop(0, ids_ref.shape[0], number, 0, unroll=4)
        scalars = pltpu.make_async_copy(idv_ref, ids_smem, id_sem)
        scalars.start()

        def zero(t, carry):
            for lt in range(2 * halves):
                for ref in (b_ref, x_ref):
                    ref[lt, pl.ds(t * 32, 32), :] = jnp.zeros((32, 128), F32)
            return carry

        lax.fori_loop(0, TILES, zero, 0)
        load.wait()
        tab_ref[192:256] = jnp.zeros((64, 2 * nc), BF16)
        for n in range(halves):
            left = slice(n * 128, n * 128 + 128)
            right = slice(nc + n * 128, nc + n * 128 + 128)
            for part in range(3):
                dr = wave_ref[n, part // 2 * 64 : part // 2 * 64 + 32]
                di = wave_ref[n, part // 2 * 64 + 32 : part // 2 * 64 + 64]
                tab_ref[part * 64 : part * 64 + 32, left] = dr
                tab_ref[part * 64 + 32 : part * 64 + 64, left] = -di
                tab_ref[part * 64 : part * 64 + 32, right] = di
                tab_ref[part * 64 + 32 : part * 64 + 64, right] = dr
        scalars.wait()

    lane = lax.broadcasted_iota(jnp.int32, (rows, 128), 1)

    def multiply(t, slot):
        p = p_ref[pl.ds(t * chunk // 2, chunk // 2)].reshape(rows, 128)
        hi = p.astype(BF16)
        hif = hi.astype(F32)
        lof = p - hif
        lo = lof.astype(BF16)
        hir = pltpu.roll(hi, 64, 1)
        lor = pltpu.roll(lo, 64, 1)
        one = jnp.where(lane < 64, hi, lor)
        two = jnp.where(lane < 64, hir, lo)
        lhs = jnp.concatenate(
            [
                jnp.concatenate([one, hi], 1),
                jnp.concatenate([two, hir], 1),
            ],
            0,
        )
        y_ref[slot] = jnp.dot(lhs, tab_ref[...], preferred_element_type=F32)

    def add(t, slot):
        for d in range(chunk):
            tile = ids_smem[g, t * chunk + d]
            r = lax.shift_right_logical(tile, shift)
            c = lax.bitwise_and(tile, TILES - 1)
            pr = jnp.broadcast_to(phr_ref[pl.ds(c, 1), :], (8, 128))
            pi = jnp.broadcast_to(phi_ref[pl.ds(c, 1), :], (8, 128))
            dst = pl.ds(pl.multiple_of(r * 32, 32), 32)
            acc = b_ref if d % 2 else x_ref
            old = acc[:, dst, :]
            y = y_ref[slot, pl.ds(d % 2 * rows + d // 2 * SUB, SUB), :]
            real, imag = [], []
            for n in range(halves):
                yr = y[:, n * 128 : n * 128 + 128].reshape(4, 8, 128)
                yi = y[:, nc + n * 128 : nc + n * 128 + 128].reshape(4, 8, 128)
                real.append((yr * pr - yi * pi).reshape(1, 32, 128))
                imag.append((yr * pi + yi * pr).reshape(1, 32, 128))
            acc[:, dst, :] = old + jnp.concatenate(real + imag, 0)

    trips = block // chunk
    multiply(0, 0)
    for t in range(trips):
        if t + 1 < trips:
            multiply(t + 1, (t + 1) % 2)
        add(t, t % 2)

    @pl.when(g == steps - 1)
    def _():
        at = lambda r, it: pl.ds(pl.multiple_of(r * 32 + it * 8, 8), 8)

        def eights(t, carry):
            n, it = t // 4, t % 4
            for b in range(16):
                xs = []
                for a in range(8):
                    pick = at(16 * a + b, it)
                    xs.append(
                        tuple(
                            x_ref[o * halves + n, pick, :] + b_ref[o * halves + n, pick, :]
                            for o in range(2)
                        )
                    )
                for k, (r, i) in enumerate(fft(xs)):
                    if b * k:
                        r, i = turn(r, i, b * k / TILES)
                    pick = at(16 * k + b, it)
                    x_ref[n, pick, :] = r
                    x_ref[halves + n, pick, :] = i
            return carry

        def sixteens(t, carry):
            n, it = t // 4, t % 4
            for a in range(8):
                xs = []
                for b in range(16):
                    pick = at(16 * a + b, it)
                    xs.append((x_ref[n, pick, :], x_ref[halves + n, pick, :]))
                for k, (r, i) in enumerate(fft(xs)):
                    pick = at(a + 8 * k, it)
                    b_ref[n, pick, :] = r
                    b_ref[halves + n, pick, :] = i
            return carry

        def mix(n, t, carry):
            parts = []
            for d in range(8):
                m = t * 8 + d
                near = pl.ds(pl.multiple_of(m * SUB, SUB), SUB)
                zh, zl = split(
                    jnp.concatenate([b_ref[o * halves + n, near, :] for o in range(2)], 0)
                )
                both = mix_ref[m]
                res = jnp.dot(
                    jnp.concatenate([both, both[:, :64]], 1),
                    jnp.concatenate([zh, zh, zl], 0),
                    preferred_element_type=F32,
                )
                parts.append(res[None])
            for q in range(8):
                block8 = jnp.concatenate([p[:, q * 8 : q * 8 + 8] for p in parts], 0)
                turned = jnp.transpose(block8, (1, 0, 2))
                for e in range(8):
                    p, b = divmod(q * 8 + e, SUB)
                    far = pl.ds(pl.multiple_of(b * TILES + t * 8, 8), 8)
                    x_ref[p * halves + n, far, :] = turned[e]
            return carry

        stores = []
        for n in range(halves):
            lax.fori_loop(4 * n, 4 * n + 4, eights, 0)
            lax.fori_loop(4 * n, 4 * n + 4, sixteens, 0)
            if n == 0:
                pltpu.make_async_copy(mix_hbm, mix_ref, mix_sem).wait()
            lax.fori_loop(0, TILES // 8, functools.partial(mix, n), 0)
            for p in range(2):
                store = pltpu.make_async_copy(
                    x_ref.at[p * halves + n],
                    out_hbm.at[p, :, pl.ds(n * 128, 128)],
                    out_sem.at[p * halves + n],
                )
                store.start()
                stores.append(store)
        for store in stores:
            store.wait()


def finish(pix, ids, phr, phi, waves, mix, nc, block):
    count = pix.shape[0] * 2
    tiles = 2 * nc // 128
    const = lambda shape: pl.BlockSpec(shape, lambda g: (0,) * len(shape))
    anywhere = pl.BlockSpec(memory_space=pl.ANY)
    x_shape = (tiles, GRID, 128)
    dma = pltpu.SemaphoreType.DMA
    return pl.pallas_call(
        functools.partial(finish_kernel, block, nc, TILES.bit_length() - 1),
        out_shape=jax.ShapeDtypeStruct((2, GRID, nc), F32),
        grid=(count // block,),
        in_specs=[
            pl.BlockSpec((block // 2, SUB, 128), lambda g: (g, 0, 0)),
            const(ids.shape),
            const(phr.shape),
            const(phi.shape),
            anywhere,
            anywhere,
        ],
        out_specs=anywhere,
        scratch_shapes=[
            pltpu.VMEM(x_shape, F32),
            pltpu.VMEM(x_shape, F32),
            pltpu.VMEM((2, 512, 2 * nc), F32),
            pltpu.VMEM((256, 2 * nc), BF16),
            pltpu.VMEM((nc // 128, 128, 128), BF16),
            pltpu.VMEM(mix.shape, BF16),
            pltpu.VMEM((count // block, 128), jnp.int32),
            pltpu.SMEM((count // block, 128), jnp.int32),
            dma,
            dma,
            dma,
            dma((tiles,)),
        ],
        name="finish",
    )(pix, ids, phr, phi, waves, mix)


def np_split(x):
    hi = x.astype(np.float32).astype(BF16)
    return hi, (x - hi.astype(np.float64)).astype(BF16)


def column_waves(g):
    waves = shifted(g) / 512.0
    rh, rl = np_split(waves.real)
    ih, il = np_split(waves.imag)
    return np.concatenate([rh, ih, rl, il], 1)


def real_form(z):
    return np.array([[z.real, -z.imag], [z.imag, z.real]])


def per_device(visibilities, offsets, vis_count, owner, tile_row, tile_col):
    wide = lax.axis_size("wide")
    nc = GRID // wide
    band = GRID // (SUB * wide)
    g, w = np_tables()
    subs = visibilities.shape[0]
    size = math.gcd(subs, 96)
    tile = ((owner * band + tile_row) * TILES + tile_col).astype(F32)
    tile = jnp.pad(tile.reshape(subs // size, 1, size), ((0, 0), (0, 7), (0, 128 - size)))
    pix, ids = gather(vis_count, visibilities, offsets, tile, wide, size)
    m4 = real_form(shifted(g) / 256.0).transpose(4, 0, 2, 1, 3).reshape(TILES, 64, 64)
    both = jnp.asarray(np.concatenate(np_split(m4), 2))
    phr, phi = jnp.asarray(w.real, F32), jnp.asarray(w.imag, F32)
    return finish(pix, ids, phr, phi, jnp.asarray(column_waves(g)), both, nc, size)


def solution(mesh):
    placed = (
        P(("group", "wide"), None, None),
        P(("group", "wide"), None, None),
        P(("group", "wide")),
        P(("group", "wide")),
        P(("group", "wide")),
        P(("group", "wide")),
    )
    return jax.shard_map(
        per_device, mesh=mesh, in_specs=placed, out_specs=P(None, "group", "wide"), check_vma=False
    )
```

```python
import functools
import math

import jax
import jax.numpy as jnp
import numpy as np
from jax import lax
from jax.experimental import pallas as pl
from jax.experimental.pallas import tpu as pltpu
from jax.sharding import PartitionSpec as P

SUB = 32
HALF = SUB // 2
VIS = 128
GRID = 4096
TILES = GRID // SUB
F32 = jnp.float32
BF16 = jnp.bfloat16


def _poly_coefs(most, degree):
    top = most**2
    nodes = top / 2 * (1 + np.cos(np.pi * (np.arange(64) + 0.5) / 64))
    r = np.sqrt(nodes)
    cheb = np.polynomial.chebyshev.Chebyshev
    c = cheb.fit(nodes, np.cos(2 * np.pi * r), degree, domain=[0, top])
    s = cheb.fit(nodes, np.sin(2 * np.pi * r) / r, degree, domain=[0, top])
    poly = np.polynomial.Polynomial
    return (
        [float(v) for v in c.convert(kind=poly).coef],
        [float(v) for v in s.convert(kind=poly).coef],
    )


ANY_TURN = _poly_coefs(0.5, 5)
SMALL_TURN = _poly_coefs((SUB / 2 - 2) / (2 * SUB), 4)


def cis(r, coefs):
    z = r * r
    c, s = coefs[0][-1], coefs[1][-1]
    for k in range(len(coefs[0]) - 2, -1, -1):
        c = c * z + coefs[0][k]
        s = s * z + coefs[1][k]
    return c, s * r


def cmul(a, b):
    return a[0] * b[0] - a[1] * b[1], a[0] * b[1] + a[1] * b[0]


def split(x):
    hi = x.astype(BF16)
    lo = (x - hi.astype(F32)).astype(BF16)
    return hi, lo


def np_tables():
    t = np.arange(SUB)
    q = np.arange(SUB)
    n0 = np.arange(TILES)
    g = np.einsum(
        "tq,qn->tn",
        np.exp(-2j * np.pi * np.outer(t, q) / SUB),
        np.exp(-2j * np.pi * np.outer(q, n0) / GRID),
    )
    w = np.exp(-2j * np.pi * (np.outer(n0, n0) % TILES) / TILES)
    return g, w


def to_waves(g):
    sign = (-1.0) ** np.arange(HALF)[None, :, None]
    up = g[:, HALF:] * sign
    down = g[:, HALF - 1 :: -1] * -sign
    return np.concatenate([up + down, 1j * (up - down)], 1)


def shifted(g):
    index = (np.arange(SUB)[:, None] + np.arange(SUB)[None, :]) % SUB
    return to_waves(g[index])


def pixel_rows(raw_ref, size, out_ref, row_ref, wave_ref):
    lane = lax.broadcasted_iota(jnp.int32, (SUB, VIS), 1)
    step = (lax.broadcasted_iota(jnp.int32, (8, VIS), 0).astype(F32) + 0.5) / SUB
    cat = jnp.concatenate

    def prepare(t):
        ar, ai, u, v = (raw_ref[q * size + t * 8 : q * size + t * 8 + 8] for q in range(4))
        first_u, first_v = (cis((x - HALF) * (1.0 / (2 * SUB)), SMALL_TURN) for x in (u, v))
        twice = cmul(first_u, first_u)
        wave = first_u
        for m in range(8):
            if m:
                wave = cmul(wave, twice)
            for part in range(2):
                row = t * 8 * 16 + part * 8 + m
                wave_ref[pl.ds(row, 8, stride=16), :] = wave[part]
        step_u = cmul(wave, first_u)
        step_v = first_v
        for _ in range(4):
            step_v = cmul(step_v, step_v)
        pr, pi = cmul(first_u, first_v)
        rows = [*step_u, *step_v, ar * pr + ai * pi, ai * pr - ar * pi, v - HALF]
        for q, row in enumerate(rows):
            row_ref[t, q] = row

    def parts(n):
        t, d = n // 8, n % 8
        bc = lambda q: jnp.broadcast_to(row_ref[t, q, d : d + 1, :], (8, VIS))
        ur, ui, vr, vi, ar, ai, v = (bc(q) for q in range(7))
        cu, su = (wave_ref[n * 16 + q * 8 : n * 16 + q * 8 + 8] for q in range(2))
        turns = v * step
        cv, sv = cis(turns - jnp.round(turns), ANY_TURN)
        ahead = lambda c, s, r, i: [c, c * r - s * i, s, c * i + s * r]
        us = ahead(cu, su, ur, ui)
        vs = ahead(cv, sv, vr, vi)
        wh, wl = split(cat([ar * x for x in us] + [ai * x for x in us], 0))
        vh, vl = split(cat(vs, 0))
        return cat([wh, wl], 1), cat([vh, vh], 1), cat([vl, vl], 1)

    def pair(n):
        one, two = parts(n), parts(n + 1)
        prod = lax.dot_general(
            cat([one[0], two[0]], 0),
            cat([one[1], two[1], one[2], two[2]], 0),
            (((1,), (1,)), ((), ())),
            preferred_element_type=F32,
        )
        ar, ai, br, bi = (prod[q * SUB : q * SUB + SUB] for q in range(4))
        fold = lambda p, q, r, s: jnp.where(
            lane < 64, jnp.where(lane < 32, p, q), jnp.where(lane < 96, r, s)
        )
        out_ref[n // 2] = fold(ar, bi, ai, br) + pltpu.roll(fold(ai, br, ar, bi), 64, 1)

    prepare(0)
    for t in range(size // 8):
        if t + 1 < size // 8:
            prepare(t + 1)
        for d in range(0, 8, 2):
            pair(t * 8 + d)


def gather_kernel(
    wide, subs, size, lag, count_ref, vis_ref, off_ref, tile_ref, pix_hbm, ids_hbm,
    raw_ref, row_ref, wave_ref, out_ref,
    send_sem, recv_sem, loc_sem, pix_send, pix_recv, id_loc, id_send, id_recv,
):
    depth = wide // 4
    pieces = subs // size
    trips = 2 * depth * pieces
    me = lax.axis_index("wide")
    core, y, z = me % 2, (me // 2) % 2, me // 4
    place = lambda zz, yy, cc: (zz * 2 + yy) * 2 + cc
    partner = {"wide": place(z, y, 1 - core)}
    across = {"wide": place(z, 1 - y, core)}
    above = {"wide": place(jnp.minimum(z + 1, depth - 1), y, core)}
    below = {"wide": place(jnp.maximum(z - 1, 0), y, core)}
    not_top, not_bottom = z < depth - 1, z > 0
    mesh_id = pl.DeviceIdType.MESH
    here = z * 2 + y

    barrier = pltpu.get_barrier_semaphore()
    for peer in (partner, across):
        pl.semaphore_signal(barrier, inc=1, device_id=peer, device_id_type=mesh_id)

    @pl.when(not_top)
    def _():
        pl.semaphore_signal(barrier, inc=1, device_id=above, device_id_type=mesh_id)

    @pl.when(not_bottom)
    def _():
        pl.semaphore_signal(barrier, inc=1, device_id=below, device_id_type=mesh_id)

    slots = lax.broadcasted_iota(jnp.int32, (2, VIS), 1)

    def stage(t, carry):
        piece = t * 8 // size
        base = t * 8 - piece * size
        for d in range(8):
            n = t * 8 + d
            live = jnp.where(slots < count_ref[n], 1.0 / math.sqrt(VIS), 0.0)
            for half, pair in enumerate((vis_ref[n] * live, off_ref[n])):
                for q in range(2):
                    row = (half * 2 + q) * size + base + d
                    raw_ref[here, piece, pl.ds(row, 1), :] = pair[q : q + 1]
        return carry

    lax.fori_loop(0, subs // 8, stage, 0)
    for piece in range(pieces):
        raw_ref[here, piece, 4 * size :, :] = tile_ref[piece]
    neighbours = jnp.minimum(z, 1) + jnp.minimum(depth - 1 - z, 1)
    pl.semaphore_wait(barrier, 2 + neighbours)

    def hop(zz, yy, piece, to, way):
        chip = zz * 2 + yy
        return pltpu.make_async_remote_copy(
            src_ref=raw_ref.at[chip, piece],
            dst_ref=raw_ref.at[chip, piece],
            send_sem=send_sem.at[zz, piece, way],
            recv_sem=recv_sem.at[chip, piece],
            device_id=to,
            device_id_type=mesh_id,
        )

    def spread_out(zz, piece, act):
        act(hop(zz, y, piece, across, 2))

        @pl.when((zz <= z) & not_top)
        def _():
            act(hop(zz, y, piece, above, 0))

        @pl.when((zz >= z) & not_bottom)
        def _():
            act(hop(zz, y, piece, below, 1))

    for piece in range(pieces):
        spread_out(z, piece, lambda copy: copy.start())

    def pass_on(number):
        far, piece = number // pieces + 1, number % pieces
        for zz, inside in ((z - far, z - far >= 0), (z + far, z + far < depth)):

            @pl.when(inside)
            def _():
                hop(zz, y, piece, across, 2).wait_recv()
                spread_out(zz, piece, lambda copy: copy.start())

    def order(k):
        near = jnp.minimum(z, depth - 1 - z)
        swing = z + ((k + 1) // 2) * (1 - 2 * (k % 2))
        edge = jnp.where(z * 2 < depth - 1, k, depth - 1 - k)
        return jnp.where(k <= 2 * near, swing, edge)

    def copies(number, chip, piece):
        rows = pl.ds(((chip * 2 + core) * subs + piece * size) // 2, size // 2)
        slot = number % 2
        mine = pltpu.make_async_copy(out_ref.at[slot], pix_hbm.at[rows], loc_sem.at[slot])
        theirs = pltpu.make_async_remote_copy(
            src_ref=out_ref.at[slot],
            dst_ref=pix_hbm.at[rows],
            send_sem=pix_send.at[slot],
            recv_sem=pix_recv.at[number],
            device_id=partner,
            device_id_type=mesh_id,
        )
        return mine, theirs

    def id_copies(number, chip, piece):
        block = raw_ref.at[chip, piece, pl.ds(4 * size, 8)]
        where = ids_hbm.at[(chip * 2 + core) * pieces + piece]
        mine = pltpu.make_async_copy(block, where, id_loc.at[number])
        theirs = pltpu.make_async_remote_copy(
            src_ref=block,
            dst_ref=where,
            send_sem=id_send.at[number],
            recv_sem=id_recv.at[number],
            device_id=partner,
            device_id_type=mesh_id,
        )
        return mine, theirs

    def body(number, carry):
        s, piece = number // pieces, number % pieces
        zz = order(s // 2)
        yy = y + (s % 2) * (1 - 2 * y)
        chip = zz * 2 + yy

        @pl.when(s % 2 == 1)
        def _():
            hop(zz, yy, piece, across, 2).wait_recv()

        for copy in id_copies(number, chip, piece):
            copy.start()

        @pl.when(number >= 2)
        def _():
            mine, theirs = copies(number, chip, piece)
            mine.wait()
            theirs.wait_send()

        pixel_rows(raw_ref.at[chip, piece], size, out_ref.at[number % 2], row_ref, wave_ref)
        for copy in copies(number, chip, piece):
            copy.start()

        @pl.when((number >= lag) & (number < lag + (depth - 1) * pieces))
        def _():
            pass_on(number - lag)

        return carry

    lax.fori_loop(0, trips, body, 0)

    def drain(number, carry):
        spread_out(number // pieces, number % pieces, lambda copy: copy.wait_send())
        return carry

    lax.fori_loop(0, depth * pieces, drain, 0)
    for number in range(2):
        mine, theirs = copies(number, here, 0)
        mine.wait()
        theirs.wait_send()

    def arrive(number, carry):
        mine, theirs = id_copies(number, here, 0)
        mine.wait()
        theirs.wait()
        copies(number, here, 0)[1].wait_recv()
        return carry

    lax.fori_loop(0, trips, arrive, 0)


def gather(counts, visibilities, offsets, tile, wide, size):
    subs = visibilities.shape[0]
    depth = wide // 4
    pieces = subs // size
    trips = 2 * depth * pieces
    dma = pltpu.SemaphoreType.DMA
    anywhere = pl.BlockSpec(memory_space=pl.ANY)
    whole = pl.BlockSpec(memory_space=pltpu.VMEM)
    return pl.pallas_call(
        functools.partial(gather_kernel, wide, subs, size, min(4, 2 * pieces - 1)),
        out_shape=[
            jax.ShapeDtypeStruct((wide * subs // 2, SUB, 128), F32),
            jax.ShapeDtypeStruct((wide * pieces, 8, 128), F32),
        ],
        in_specs=[pl.BlockSpec(memory_space=pltpu.SMEM), whole, whole, whole],
        out_specs=[anywhere, anywhere],
        scratch_shapes=[
            pltpu.VMEM((wide // 2, pieces, 4 * size + 8, 128), F32),
            pltpu.VMEM((size // 8, 7, 8, VIS), F32),
            pltpu.VMEM((size * 16, VIS), F32),
            pltpu.VMEM((2, size // 2, SUB, 128), F32),
            dma((depth, pieces, 3)),
            dma((wide // 2, pieces)),
            dma((2,)),
            dma((2,)),
            dma((trips,)),
            dma((trips,)),
            dma((trips,)),
            dma((trips,)),
        ],
        compiler_params=pltpu.CompilerParams(collective_id=0, has_side_effects=True),
        name="gather",
    )(counts, visibilities, offsets, tile)


def fft(xs):
    n = len(xs)
    if n == 1:
        return xs
    even, odd = fft(xs[::2]), fft(xs[1::2])
    low, high = [], []
    root = math.sqrt(0.5)
    for k, ((er, ei), (r, i)) in enumerate(zip(even, odd)):
        if k == 0:
            tr, ti = r, i
        elif 4 * k == n:
            low.append((er + i, ei - r))
            high.append((er - i, ei + r))
            continue
        elif 8 * k == n:
            tr, ti = (r + i) * root, (i - r) * root
        elif 8 * k == 3 * n:
            tr, ti = (i - r) * root, (r + i) * -root
        else:
            tr, ti = turn(r, i, k / n)
        low.append((er + tr, ei + ti))
        high.append((er - tr, ei - ti))
    return low + high


def turn(r, i, turns):
    c, s = math.cos(2 * math.pi * turns), math.sin(2 * math.pi * turns)
    return r * c + i * s, i * c - r * s


def finish_kernel(
    block, nc, shift, p_ref, ids_ref, phr_ref, phi_ref, waves_hbm, mix_hbm, out_hbm,
    x_ref, b_ref, y_ref, tab_ref, wave_ref, mix_ref, idv_ref, ids_smem, sem, id_sem, mix_sem, out_sem,
):
    g = pl.program_id(0)
    steps = pl.num_programs(0)
    halves = nc // 128
    chunk = 16
    rows = chunk * 16

    @pl.when(g == 0)
    def _():
        first = lax.axis_index("wide") * halves
        pltpu.make_async_copy(mix_hbm, mix_ref, mix_sem).start()
        load = pltpu.make_async_copy(waves_hbm.at[pl.ds(first, halves)], wave_ref, sem)
        load.start()

        def number(t, carry):
            idv_ref[pl.ds(t, 1), :] = ids_ref[t, 0:1, :].astype(jnp.int32)
            return carry

        lax.fori_loop(0, ids_ref.shape[0], number, 0, unroll=4)
        scalars = pltpu.make_async_copy(idv_ref, ids_smem, id_sem)
        scalars.start()

        def zero(t, carry):
            for lt in range(2 * halves):
                for ref in (b_ref, x_ref):
                    ref[lt, pl.ds(t * 32, 32), :] = jnp.zeros((32, 128), F32)
            return carry

        lax.fori_loop(0, TILES, zero, 0)
        load.wait()
        tab_ref[...] = jnp.zeros(tab_ref.shape, BF16)
        for n in range(halves):
            left = slice(n * 128, n * 128 + 128)
            right = slice(nc + n * 128, nc + n * 128 + 128)
            for row, low in ((0, 0), (32, 0), (128, 64)):
                dr = wave_ref[n, low : low + 32]
                di = wave_ref[n, low + 32 : low + 64]
                tab_ref[row : row + 32, left] = dr
                tab_ref[row : row + 32, right] = di
                tab_ref[row + 64 : row + 96, left] = -di
                tab_ref[row + 64 : row + 96, right] = dr
        scalars.wait()

    early = lax.broadcasted_iota(jnp.int32, (rows, 128), 1) % 64 < 32

    def multiply(t, slot):
        p = p_ref[pl.ds(t * chunk // 2, chunk // 2)].reshape(rows, 128)
        hi = p.astype(BF16)
        hif = hi.astype(F32)
        lof = p - hif
        lo = lof.astype(BF16)
        hir = pltpu.roll(hi, 32, 1)
        one = jnp.where(early, hi, pltpu.roll(lo, 32, 1))
        two = jnp.where(early, hir, pltpu.roll(lo, 64, 1))
        lhs = jnp.concatenate(
            [
                jnp.concatenate([one, hi], 1),
                jnp.concatenate([two, hir], 1),
            ],
            0,
        )
        y_ref[slot] = jnp.dot(lhs, tab_ref[...], preferred_element_type=F32)

    def add(t, slot):
        for d in range(chunk):
            tile = ids_smem[g, t * chunk + d]
            r = lax.shift_right_logical(tile, shift)
            c = lax.bitwise_and(tile, TILES - 1)
            pr = jnp.broadcast_to(phr_ref[pl.ds(c, 1), :], (8, 128))
            pi = jnp.broadcast_to(phi_ref[pl.ds(c, 1), :], (8, 128))
            dst = pl.ds(pl.multiple_of(r * 32, 32), 32)
            acc = b_ref if d % 2 else x_ref
            old = acc[:, dst, :]
            y = y_ref[slot, pl.ds(d % 2 * rows + d // 2 * SUB, SUB), :]
            real, imag = [], []
            for n in range(halves):
                yr = y[:, n * 128 : n * 128 + 128].reshape(4, 8, 128)
                yi = y[:, nc + n * 128 : nc + n * 128 + 128].reshape(4, 8, 128)
                real.append((yr * pr - yi * pi).reshape(1, 32, 128))
                imag.append((yr * pi + yi * pr).reshape(1, 32, 128))
            acc[:, dst, :] = old + jnp.concatenate(real + imag, 0)

    trips = block // chunk
    multiply(0, 0)
    for t in range(trips):
        if t + 1 < trips:
            multiply(t + 1, (t + 1) % 2)
        add(t, t % 2)

    @pl.when(g == steps - 1)
    def _():
        at = lambda r, it: pl.ds(pl.multiple_of(r * 32 + it * 8, 8), 8)

        def eights(t, carry):
            n, it = t // 4, t % 4
            for b in range(16):
                xs = []
                for a in range(8):
                    pick = at(16 * a + b, it)
                    xs.append(
                        tuple(
                            x_ref[o * halves + n, pick, :] + b_ref[o * halves + n, pick, :]
                            for o in range(2)
                        )
                    )
                for k, (r, i) in enumerate(fft(xs)):
                    if b * k:
                        r, i = turn(r, i, b * k / TILES)
                    pick = at(16 * k + b, it)
                    x_ref[n, pick, :] = r
                    x_ref[halves + n, pick, :] = i
            return carry

        def sixteens(t, carry):
            n, it = t // 4, t % 4
            for a in range(8):
                xs = []
                for b in range(16):
                    pick = at(16 * a + b, it)
                    xs.append((x_ref[n, pick, :], x_ref[halves + n, pick, :]))
                for k, (r, i) in enumerate(fft(xs)):
                    pick = at(a + 8 * k, it)
                    b_ref[n, pick, :] = r
                    b_ref[halves + n, pick, :] = i
            return carry

        def mix(n, t, carry):
            parts = []
            for d in range(8):
                m = t * 8 + d
                near = pl.ds(pl.multiple_of(m * SUB, SUB), SUB)
                zh, zl = split(
                    jnp.concatenate([b_ref[o * halves + n, near, :] for o in range(2)], 0)
                )
                both = mix_ref[m]
                res = jnp.dot(
                    jnp.concatenate([both, both[:, :64]], 1),
                    jnp.concatenate([zh, zh, zl], 0),
                    preferred_element_type=F32,
                )
                parts.append(res[None])
            for q in range(8):
                block8 = jnp.concatenate([p[:, q * 8 : q * 8 + 8] for p in parts], 0)
                turned = jnp.transpose(block8, (1, 0, 2))
                for e in range(8):
                    p, b = divmod(q * 8 + e, SUB)
                    far = pl.ds(pl.multiple_of(b * TILES + t * 8, 8), 8)
                    x_ref[p * halves + n, far, :] = turned[e]
            return carry

        stores = []
        for n in range(halves):
            lax.fori_loop(4 * n, 4 * n + 4, eights, 0)
            lax.fori_loop(4 * n, 4 * n + 4, sixteens, 0)
            if n == 0:
                pltpu.make_async_copy(mix_hbm, mix_ref, mix_sem).wait()
            lax.fori_loop(0, TILES // 8, functools.partial(mix, n), 0)
            for p in range(2):
                store = pltpu.make_async_copy(
                    x_ref.at[p * halves + n],
                    out_hbm.at[p, :, pl.ds(n * 128, 128)],
                    out_sem.at[p * halves + n],
                )
                store.start()
                stores.append(store)
        for store in stores:
            store.wait()


def finish(pix, ids, phr, phi, waves, mix, nc, block):
    count = pix.shape[0] * 2
    tiles = 2 * nc // 128
    const = lambda shape: pl.BlockSpec(shape, lambda g: (0,) * len(shape))
    anywhere = pl.BlockSpec(memory_space=pl.ANY)
    x_shape = (tiles, GRID, 128)
    dma = pltpu.SemaphoreType.DMA
    return pl.pallas_call(
        functools.partial(finish_kernel, block, nc, TILES.bit_length() - 1),
        out_shape=jax.ShapeDtypeStruct((2, GRID, nc), F32),
        grid=(count // block,),
        in_specs=[
            pl.BlockSpec((block // 2, SUB, 128), lambda g: (g, 0, 0)),
            const(ids.shape),
            const(phr.shape),
            const(phi.shape),
            anywhere,
            anywhere,
        ],
        out_specs=anywhere,
        scratch_shapes=[
            pltpu.VMEM(x_shape, F32),
            pltpu.VMEM(x_shape, F32),
            pltpu.VMEM((2, 512, 2 * nc), F32),
            pltpu.VMEM((256, 2 * nc), BF16),
            pltpu.VMEM((nc // 128, 128, 128), BF16),
            pltpu.VMEM(mix.shape, BF16),
            pltpu.VMEM((count // block, 128), jnp.int32),
            pltpu.SMEM((count // block, 128), jnp.int32),
            dma,
            dma,
            dma,
            dma((tiles,)),
        ],
        name="finish",
    )(pix, ids, phr, phi, waves, mix)


def np_split(x):
    hi = x.astype(np.float32).astype(BF16)
    return hi, (x - hi.astype(np.float64)).astype(BF16)


def column_waves(g):
    waves = shifted(g) / 512.0
    rh, rl = np_split(waves.real)
    ih, il = np_split(waves.imag)
    return np.concatenate([rh, ih, rl, il], 1)


def real_form(z):
    return np.array([[z.real, -z.imag], [z.imag, z.real]])


def per_device(visibilities, offsets, vis_count, owner, tile_row, tile_col):
    wide = lax.axis_size("wide")
    nc = GRID // wide
    band = GRID // (SUB * wide)
    g, w = np_tables()
    subs = visibilities.shape[0]
    size = math.gcd(subs, 96)
    tile = ((owner * band + tile_row) * TILES + tile_col).astype(F32)
    tile = jnp.pad(tile.reshape(subs // size, 1, size), ((0, 0), (0, 7), (0, 128 - size)))
    pix, ids = gather(vis_count, visibilities, offsets, tile, wide, size)
    m4 = real_form(shifted(g) / 256.0).transpose(4, 0, 2, 1, 3).reshape(TILES, 64, 64)
    both = jnp.asarray(np.concatenate(np_split(m4), 2))
    phr, phi = jnp.asarray(w.real, F32), jnp.asarray(w.imag, F32)
    return finish(pix, ids, phr, phi, jnp.asarray(column_waves(g)), both, nc, size)


def solution(mesh):
    placed = (
        P(("group", "wide"), None, None),
        P(("group", "wide"), None, None),
        P(("group", "wide")),
        P(("group", "wide")),
        P(("group", "wide")),
        P(("group", "wide")),
    )
    return jax.shard_map(
        per_device, mesh=mesh, in_specs=placed, out_specs=P(None, "group", "wide"), check_vma=False
    )
```

```python
import functools
import math

import jax
import jax.numpy as jnp
import numpy as np
from jax import lax
from jax.experimental import pallas as pl
from jax.experimental.pallas import tpu as pltpu
from jax.sharding import PartitionSpec as P

SUB = 32
HALF = SUB // 2
VIS = 128
GRID = 4096
TILES = GRID // SUB
F32 = jnp.float32
BF16 = jnp.bfloat16


def _poly_coefs(most, degree):
    top = most**2
    nodes = top / 2 * (1 + np.cos(np.pi * (np.arange(64) + 0.5) / 64))
    r = np.sqrt(nodes)
    cheb = np.polynomial.chebyshev.Chebyshev
    c = cheb.fit(nodes, np.cos(2 * np.pi * r), degree, domain=[0, top])
    s = cheb.fit(nodes, np.sin(2 * np.pi * r) / r, degree, domain=[0, top])
    poly = np.polynomial.Polynomial
    return (
        [float(v) for v in c.convert(kind=poly).coef],
        [float(v) for v in s.convert(kind=poly).coef],
    )


ANY_TURN = _poly_coefs(0.5, 5)
SMALL_TURN = _poly_coefs((SUB / 2 - 2) / (2 * SUB), 4)


def cis(r, coefs):
    z = r * r
    c, s = coefs[0][-1], coefs[1][-1]
    for k in range(len(coefs[0]) - 2, -1, -1):
        c = c * z + coefs[0][k]
        s = s * z + coefs[1][k]
    return c, s * r


def cmul(a, b):
    return a[0] * b[0] - a[1] * b[1], a[0] * b[1] + a[1] * b[0]


def split(x):
    hi = x.astype(BF16)
    lo = (x - hi.astype(F32)).astype(BF16)
    return hi, lo


def np_tables():
    t = np.arange(SUB)
    q = np.arange(SUB)
    n0 = np.arange(TILES)
    g = np.einsum(
        "tq,qn->tn",
        np.exp(-2j * np.pi * np.outer(t, q) / SUB),
        np.exp(-2j * np.pi * np.outer(q, n0) / GRID),
    )
    w = np.exp(-2j * np.pi * (np.outer(n0, n0) % TILES) / TILES)
    return g, w


def to_waves(g):
    sign = (-1.0) ** np.arange(HALF)[None, :, None]
    up = g[:, HALF:] * sign
    down = g[:, HALF - 1 :: -1] * -sign
    return np.concatenate([up + down, 1j * (up - down)], 1)


def shifted(g):
    index = (np.arange(SUB)[:, None] + np.arange(SUB)[None, :]) % SUB
    return to_waves(g[index])


def pixel_rows(raw_ref, size, out_ref, row_ref, wave_ref):
    lane = lax.broadcasted_iota(jnp.int32, (SUB, VIS), 1)
    step = (lax.broadcasted_iota(jnp.int32, (8, VIS), 0).astype(F32) + 0.5) / SUB
    cat = jnp.concatenate

    def prepare(t):
        ar, ai, u, v = (raw_ref[q * size + t * 8 : q * size + t * 8 + 8] for q in range(4))
        first_u, first_v = (cis((x - HALF) * (1.0 / (2 * SUB)), SMALL_TURN) for x in (u, v))
        twice = cmul(first_u, first_u)
        wave = first_u
        for m in range(8):
            if m:
                wave = cmul(wave, twice)
            for part in range(2):
                row = t * 8 * 16 + part * 8 + m
                wave_ref[pl.ds(row, 8, stride=16), :] = wave[part]
        step_u = cmul(wave, first_u)
        step_v = first_v
        for _ in range(4):
            step_v = cmul(step_v, step_v)
        pr, pi = cmul(first_u, first_v)
        rows = [*step_u, *step_v, ar * pr + ai * pi, ai * pr - ar * pi, v - HALF]
        for q, row in enumerate(rows):
            row_ref[t, q] = row

    def parts(n):
        t, d = n // 8, n % 8
        bc = lambda q: jnp.broadcast_to(row_ref[t, q, d : d + 1, :], (8, VIS))
        ur, ui, vr, vi, ar, ai, v = (bc(q) for q in range(7))
        cu, su = (wave_ref[n * 16 + q * 8 : n * 16 + q * 8 + 8] for q in range(2))
        turns = v * step
        cv, sv = cis(turns - jnp.round(turns), ANY_TURN)
        ahead = lambda c, s, r, i: [c, c * r - s * i, s, c * i + s * r]
        us = ahead(cu, su, ur, ui)
        vs = ahead(cv, sv, vr, vi)
        wh, wl = split(cat([ar * x for x in us] + [ai * x for x in us], 0))
        vh, vl = split(cat(vs, 0))
        return cat([wh, wl], 1), cat([vh, vh], 1), cat([vl, vl], 1)

    def pair(n):
        one, two = parts(n), parts(n + 1)
        prod = lax.dot_general(
            cat([one[0], two[0]], 0),
            cat([one[1], two[1], one[2], two[2]], 0),
            (((1,), (1,)), ((), ())),
            preferred_element_type=F32,
        )
        ar, ai, br, bi = (prod[q * SUB : q * SUB + SUB] for q in range(4))
        fold = lambda p, q, r, s: jnp.where(
            lane < 64, jnp.where(lane < 32, p, q), jnp.where(lane < 96, r, s)
        )
        out_ref[n // 2] = fold(ar, bi, ai, br) + pltpu.roll(fold(ai, br, ar, bi), 64, 1)

    prepare(0)
    for t in range(size // 8):
        if t + 1 < size // 8:
            prepare(t + 1)
        for d in range(0, 8, 2):
            pair(t * 8 + d)


def gather_kernel(
    wide, subs, size, count_ref, vis_ref, off_ref, tile_ref, pix_hbm, ids_hbm,
    raw_ref, row_ref, wave_ref, out_ref,
    send_sem, recv_sem, loc_sem, pix_send, pix_recv, id_loc, id_send, id_recv,
):
    depth = wide // 4
    pieces = subs // size
    trips = 2 * depth * pieces
    relays = (depth - 1) * pieces
    me = lax.axis_index("wide")
    core, y, z = me % 2, (me // 2) % 2, me // 4
    place = lambda zz, yy, cc: (zz * 2 + yy) * 2 + cc
    partner = {"wide": place(z, y, 1 - core)}
    across = {"wide": place(z, 1 - y, core)}
    above = {"wide": place(jnp.minimum(z + 1, depth - 1), y, core)}
    below = {"wide": place(jnp.maximum(z - 1, 0), y, core)}
    not_top, not_bottom = z < depth - 1, z > 0
    mesh_id = pl.DeviceIdType.MESH
    here = z * 2 + y

    barrier = pltpu.get_barrier_semaphore()
    for peer in (partner, across):
        pl.semaphore_signal(barrier, inc=1, device_id=peer, device_id_type=mesh_id)

    @pl.when(not_top)
    def _():
        pl.semaphore_signal(barrier, inc=1, device_id=above, device_id_type=mesh_id)

    @pl.when(not_bottom)
    def _():
        pl.semaphore_signal(barrier, inc=1, device_id=below, device_id_type=mesh_id)

    slots = lax.broadcasted_iota(jnp.int32, (2, VIS), 1)

    def stage(t, carry):
        piece = t * 8 // size
        base = t * 8 - piece * size
        for d in range(8):
            n = t * 8 + d
            live = jnp.where(slots < count_ref[n], 1.0 / math.sqrt(VIS), 0.0)
            for half, pair in enumerate((vis_ref[n] * live, off_ref[n])):
                for q in range(2):
                    row = (half * 2 + q) * size + base + d
                    raw_ref[here, piece, pl.ds(row, 1), :] = pair[q : q + 1]
        return carry

    lax.fori_loop(0, subs // 8, stage, 0)
    for piece in range(pieces):
        raw_ref[here, piece, 4 * size :, :] = tile_ref[piece]
    neighbours = jnp.minimum(z, 1) + jnp.minimum(depth - 1 - z, 1)
    pl.semaphore_wait(barrier, 2 + neighbours)

    def hop(zz, yy, piece, to, way):
        chip = zz * 2 + yy
        return pltpu.make_async_remote_copy(
            src_ref=raw_ref.at[chip, piece],
            dst_ref=raw_ref.at[chip, piece],
            send_sem=send_sem.at[zz, piece, way],
            recv_sem=recv_sem.at[chip, piece],
            device_id=to,
            device_id_type=mesh_id,
        )

    def spread_out(zz, piece, act):
        act(hop(zz, y, piece, across, 2))

        @pl.when((zz <= z) & not_top)
        def _():
            act(hop(zz, y, piece, above, 0))

        @pl.when((zz >= z) & not_bottom)
        def _():
            act(hop(zz, y, piece, below, 1))

    for piece in range(pieces):
        spread_out(z, piece, lambda copy: copy.start())

    def pass_on(number):
        far, piece = number // pieces + 1, number % pieces
        for zz, inside in ((z - far, z - far >= 0), (z + far, z + far < depth)):

            @pl.when(inside)
            def _():
                hop(zz, y, piece, across, 2).wait_recv()
                spread_out(zz, piece, lambda copy: copy.start())

    def order(k):
        near = jnp.minimum(z, depth - 1 - z)
        swing = z + ((k + 1) // 2) * (1 - 2 * (k % 2))
        edge = jnp.where(z * 2 < depth - 1, k, depth - 1 - k)
        return jnp.where(k <= 2 * near, swing, edge)

    def copies(number, chip, piece):
        rows = pl.ds(((chip * 2 + core) * subs + piece * size) // 2, size // 2)
        slot = number % 2
        mine = pltpu.make_async_copy(out_ref.at[slot], pix_hbm.at[rows], loc_sem.at[slot])
        theirs = pltpu.make_async_remote_copy(
            src_ref=out_ref.at[slot],
            dst_ref=pix_hbm.at[rows],
            send_sem=pix_send.at[slot],
            recv_sem=pix_recv.at[number],
            device_id=partner,
            device_id_type=mesh_id,
        )
        return mine, theirs

    def id_copies(number, chip, piece):
        block = raw_ref.at[chip, piece, pl.ds(4 * size, 8)]
        where = ids_hbm.at[(chip * 2 + core) * pieces + piece]
        mine = pltpu.make_async_copy(block, where, id_loc.at[number])
        theirs = pltpu.make_async_remote_copy(
            src_ref=block,
            dst_ref=where,
            send_sem=id_send.at[number],
            recv_sem=id_recv.at[number],
            device_id=partner,
            device_id_type=mesh_id,
        )
        return mine, theirs

    def body(number, carry):
        later = number - pieces
        middle, end = later // 2, later - 2 * relays
        in_middle, in_end = later >= 0, end >= 0
        k = jnp.where(in_end, depth - 1, jnp.where(in_middle, middle // pieces + later % 2, 0))
        piece = jnp.where(in_end, end, jnp.where(in_middle, middle % pieces, number))
        other = jnp.where(in_end, 1, jnp.where(in_middle, 1 - later % 2, 0))
        zz = order(k)
        yy = y + other * (1 - 2 * y)
        chip = zz * 2 + yy

        @pl.when(other == 1)
        def _():
            hop(zz, yy, piece, across, 2).wait_recv()

        for copy in id_copies(number, chip, piece):
            copy.start()

        @pl.when(number >= 2)
        def _():
            mine, theirs = copies(number, chip, piece)
            mine.wait()
            theirs.wait_send()

        pixel_rows(raw_ref.at[chip, piece], size, out_ref.at[number % 2], row_ref, wave_ref)
        for copy in copies(number, chip, piece):
            copy.start()

        @pl.when((number % 2 == 1) & (number // 2 < relays))
        def _():
            pass_on(number // 2)

        return carry

    lax.fori_loop(0, trips, body, 0)

    def drain(number, carry):
        spread_out(number // pieces, number % pieces, lambda copy: copy.wait_send())
        return carry

    lax.fori_loop(0, depth * pieces, drain, 0)
    for number in range(2):
        mine, theirs = copies(number, here, 0)
        mine.wait()
        theirs.wait_send()

    def arrive(number, carry):
        mine, theirs = id_copies(number, here, 0)
        mine.wait()
        theirs.wait()
        copies(number, here, 0)[1].wait_recv()
        return carry

    lax.fori_loop(0, trips, arrive, 0)


def gather(counts, visibilities, offsets, tile, wide, size):
    subs = visibilities.shape[0]
    depth = wide // 4
    pieces = subs // size
    trips = 2 * depth * pieces
    dma = pltpu.SemaphoreType.DMA
    anywhere = pl.BlockSpec(memory_space=pl.ANY)
    whole = pl.BlockSpec(memory_space=pltpu.VMEM)
    return pl.pallas_call(
        functools.partial(gather_kernel, wide, subs, size),
        out_shape=[
            jax.ShapeDtypeStruct((wide * subs // 2, SUB, 128), F32),
            jax.ShapeDtypeStruct((wide * pieces, 8, 128), F32),
        ],
        in_specs=[pl.BlockSpec(memory_space=pltpu.SMEM), whole, whole, whole],
        out_specs=[anywhere, anywhere],
        scratch_shapes=[
            pltpu.VMEM((wide // 2, pieces, 4 * size + 8, 128), F32),
            pltpu.VMEM((size // 8, 7, 8, VIS), F32),
            pltpu.VMEM((size * 16, VIS), F32),
            pltpu.VMEM((2, size // 2, SUB, 128), F32),
            dma((depth, pieces, 3)),
            dma((wide // 2, pieces)),
            dma((2,)),
            dma((2,)),
            dma((trips,)),
            dma((trips,)),
            dma((trips,)),
            dma((trips,)),
        ],
        compiler_params=pltpu.CompilerParams(collective_id=0, has_side_effects=True),
        name="gather",
    )(counts, visibilities, offsets, tile)


def fft(xs):
    n = len(xs)
    if n == 1:
        return xs
    even, odd = fft(xs[::2]), fft(xs[1::2])
    low, high = [], []
    root = math.sqrt(0.5)
    for k, ((er, ei), (r, i)) in enumerate(zip(even, odd)):
        if k == 0:
            tr, ti = r, i
        elif 4 * k == n:
            low.append((er + i, ei - r))
            high.append((er - i, ei + r))
            continue
        elif 8 * k == n:
            tr, ti = (r + i) * root, (i - r) * root
        elif 8 * k == 3 * n:
            tr, ti = (i - r) * root, (r + i) * -root
        else:
            tr, ti = turn(r, i, k / n)
        low.append((er + tr, ei + ti))
        high.append((er - tr, ei - ti))
    return low + high


def turn(r, i, turns):
    c, s = math.cos(2 * math.pi * turns), math.sin(2 * math.pi * turns)
    return r * c + i * s, i * c - r * s


def finish_kernel(
    block, size, nc, shift, p_ref, ids_ref, phr_ref, phi_ref, waves_hbm, mix_hbm, out_hbm,
    x_ref, b_ref, y_ref, tab_ref, wave_ref, mix_ref, idv_ref, ids_smem, sem, id_sem, mix_sem, out_sem,
):
    g = pl.program_id(0)
    steps = pl.num_programs(0)
    halves = nc // 128
    chunk = 16
    rows = chunk * 16

    @pl.when(g == 0)
    def _():
        first = lax.axis_index("wide") * halves
        pltpu.make_async_copy(mix_hbm, mix_ref, mix_sem).start()
        load = pltpu.make_async_copy(waves_hbm.at[pl.ds(first, halves)], wave_ref, sem)
        load.start()

        def number(t, carry):
            idv_ref[pl.ds(t, 1), :] = ids_ref[t, 0:1, :].astype(jnp.int32)
            return carry

        lax.fori_loop(0, ids_ref.shape[0], number, 0, unroll=4)
        scalars = pltpu.make_async_copy(idv_ref, ids_smem, id_sem)
        scalars.start()

        def zero(t, carry):
            for lt in range(2 * halves):
                for ref in (b_ref, x_ref):
                    ref[lt, pl.ds(t * 32, 32), :] = jnp.zeros((32, 128), F32)
            return carry

        lax.fori_loop(0, TILES, zero, 0)
        load.wait()
        tab_ref[...] = jnp.zeros(tab_ref.shape, BF16)
        for n in range(halves):
            left = slice(n * 128, n * 128 + 128)
            right = slice(nc + n * 128, nc + n * 128 + 128)
            for row, low in ((0, 0), (32, 0), (128, 64)):
                dr = wave_ref[n, low : low + 32]
                di = wave_ref[n, low + 32 : low + 64]
                tab_ref[row : row + 32, left] = dr
                tab_ref[row : row + 32, right] = di
                tab_ref[row + 64 : row + 96, left] = -di
                tab_ref[row + 64 : row + 96, right] = dr
        scalars.wait()

    early = lax.broadcasted_iota(jnp.int32, (rows, 128), 1) % 64 < 32

    def multiply(t, slot):
        p = p_ref[pl.ds(t * chunk // 2, chunk // 2)].reshape(rows, 128)
        hi = p.astype(BF16)
        hif = hi.astype(F32)
        lof = p - hif
        lo = lof.astype(BF16)
        hir = pltpu.roll(hi, 32, 1)
        one = jnp.where(early, hi, pltpu.roll(lo, 32, 1))
        two = jnp.where(early, hir, pltpu.roll(lo, 64, 1))
        lhs = jnp.concatenate(
            [
                jnp.concatenate([one, hi], 1),
                jnp.concatenate([two, hir], 1),
            ],
            0,
        )
        y_ref[slot] = jnp.dot(lhs, tab_ref[...], preferred_element_type=F32)

    def add(t, slot):
        for d in range(chunk):
            at = t * chunk + d
            tile = ids_smem[g * (block // size) + at // size, at % size]
            r = lax.shift_right_logical(tile, shift)
            c = lax.bitwise_and(tile, TILES - 1)
            pr = jnp.broadcast_to(phr_ref[pl.ds(c, 1), :], (8, 128))
            pi = jnp.broadcast_to(phi_ref[pl.ds(c, 1), :], (8, 128))
            dst = pl.ds(pl.multiple_of(r * 32, 32), 32)
            acc = b_ref if d % 2 else x_ref
            old = acc[:, dst, :]
            y = y_ref[slot, pl.ds(d % 2 * rows + d // 2 * SUB, SUB), :]
            real, imag = [], []
            for n in range(halves):
                yr = y[:, n * 128 : n * 128 + 128].reshape(4, 8, 128)
                yi = y[:, nc + n * 128 : nc + n * 128 + 128].reshape(4, 8, 128)
                real.append((yr * pr - yi * pi).reshape(1, 32, 128))
                imag.append((yr * pi + yi * pr).reshape(1, 32, 128))
            acc[:, dst, :] = old + jnp.concatenate(real + imag, 0)

    trips = block // chunk
    multiply(0, 0)
    for t in range(trips):
        if t + 1 < trips:
            multiply(t + 1, (t + 1) % 2)
        add(t, t % 2)

    @pl.when(g == steps - 1)
    def _():
        at = lambda r, it: pl.ds(pl.multiple_of(r * 32 + it * 8, 8), 8)

        def eights(t, carry):
            n, it = t // 4, t % 4
            for b in range(16):
                xs = []
                for a in range(8):
                    pick = at(16 * a + b, it)
                    xs.append(
                        tuple(
                            x_ref[o * halves + n, pick, :] + b_ref[o * halves + n, pick, :]
                            for o in range(2)
                        )
                    )
                for k, (r, i) in enumerate(fft(xs)):
                    if b * k:
                        r, i = turn(r, i, b * k / TILES)
                    pick = at(16 * k + b, it)
                    x_ref[n, pick, :] = r
                    x_ref[halves + n, pick, :] = i
            return carry

        def sixteens(t, carry):
            n, it = t // 4, t % 4
            for a in range(8):
                xs = []
                for b in range(16):
                    pick = at(16 * a + b, it)
                    xs.append((x_ref[n, pick, :], x_ref[halves + n, pick, :]))
                for k, (r, i) in enumerate(fft(xs)):
                    pick = at(a + 8 * k, it)
                    b_ref[n, pick, :] = r
                    b_ref[halves + n, pick, :] = i
            return carry

        def mix(n, t, carry):
            parts = []
            for d in range(8):
                m = t * 8 + d
                near = pl.ds(pl.multiple_of(m * SUB, SUB), SUB)
                zh, zl = split(
                    jnp.concatenate([b_ref[o * halves + n, near, :] for o in range(2)], 0)
                )
                both = mix_ref[m]
                res = jnp.dot(
                    jnp.concatenate([both, both[:, :64]], 1),
                    jnp.concatenate([zh, zh, zl], 0),
                    preferred_element_type=F32,
                )
                parts.append(res[None])
            for q in range(8):
                block8 = jnp.concatenate([p[:, q * 8 : q * 8 + 8] for p in parts], 0)
                turned = jnp.transpose(block8, (1, 0, 2))
                for e in range(8):
                    p, b = divmod(q * 8 + e, SUB)
                    far = pl.ds(pl.multiple_of(b * TILES + t * 8, 8), 8)
                    x_ref[p * halves + n, far, :] = turned[e]
            return carry

        stores = []
        for n in range(halves):
            lax.fori_loop(4 * n, 4 * n + 4, eights, 0)
            lax.fori_loop(4 * n, 4 * n + 4, sixteens, 0)
            if n == 0:
                pltpu.make_async_copy(mix_hbm, mix_ref, mix_sem).wait()
            lax.fori_loop(0, TILES // 8, functools.partial(mix, n), 0)
            for p in range(2):
                store = pltpu.make_async_copy(
                    x_ref.at[p * halves + n],
                    out_hbm.at[p, :, pl.ds(n * 128, 128)],
                    out_sem.at[p * halves + n],
                )
                store.start()
                stores.append(store)
        for store in stores:
            store.wait()


def finish(pix, ids, phr, phi, waves, mix, nc, size):
    count = pix.shape[0] * 2
    block = math.gcd(count, 2 * size)
    tiles = 2 * nc // 128
    const = lambda shape: pl.BlockSpec(shape, lambda g: (0,) * len(shape))
    anywhere = pl.BlockSpec(memory_space=pl.ANY)
    x_shape = (tiles, GRID, 128)
    dma = pltpu.SemaphoreType.DMA
    return pl.pallas_call(
        functools.partial(finish_kernel, block, size, nc, TILES.bit_length() - 1),
        out_shape=jax.ShapeDtypeStruct((2, GRID, nc), F32),
        grid=(count // block,),
        in_specs=[
            pl.BlockSpec((block // 2, SUB, 128), lambda g: (g, 0, 0)),
            const(ids.shape),
            const(phr.shape),
            const(phi.shape),
            anywhere,
            anywhere,
        ],
        out_specs=anywhere,
        scratch_shapes=[
            pltpu.VMEM(x_shape, F32),
            pltpu.VMEM(x_shape, F32),
            pltpu.VMEM((2, 512, 2 * nc), F32),
            pltpu.VMEM((256, 2 * nc), BF16),
            pltpu.VMEM((nc // 128, 128, 128), BF16),
            pltpu.VMEM(mix.shape, BF16),
            pltpu.VMEM((count // size, 128), jnp.int32),
            pltpu.SMEM((count // size, 128), jnp.int32),
            dma,
            dma,
            dma,
            dma((tiles,)),
        ],
        name="finish",
    )(pix, ids, phr, phi, waves, mix)


def np_split(x):
    hi = x.astype(np.float32).astype(BF16)
    return hi, (x - hi.astype(np.float64)).astype(BF16)


def column_waves(g):
    waves = shifted(g) / 512.0
    rh, rl = np_split(waves.real)
    ih, il = np_split(waves.imag)
    return np.concatenate([rh, ih, rl, il], 1)


def real_form(z):
    return np.array([[z.real, -z.imag], [z.imag, z.real]])


def per_device(visibilities, offsets, vis_count, owner, tile_row, tile_col):
    wide = lax.axis_size("wide")
    nc = GRID // wide
    band = GRID // (SUB * wide)
    g, w = np_tables()
    subs = visibilities.shape[0]
    size = math.gcd(subs, 96)
    tile = ((owner * band + tile_row) * TILES + tile_col).astype(F32)
    tile = jnp.pad(tile.reshape(subs // size, 1, size), ((0, 0), (0, 7), (0, 128 - size)))
    pix, ids = gather(vis_count, visibilities, offsets, tile, wide, size)
    m4 = real_form(shifted(g) / 256.0).transpose(4, 0, 2, 1, 3).reshape(TILES, 64, 64)
    both = jnp.asarray(np.concatenate(np_split(m4), 2))
    phr, phi = jnp.asarray(w.real, F32), jnp.asarray(w.imag, F32)
    return finish(pix, ids, phr, phi, jnp.asarray(column_waves(g)), both, nc, size)


def solution(mesh):
    placed = (
        P(("group", "wide"), None, None),
        P(("group", "wide"), None, None),
        P(("group", "wide")),
        P(("group", "wide")),
        P(("group", "wide")),
        P(("group", "wide")),
    )
    return jax.shard_map(
        per_device, mesh=mesh, in_specs=placed, out_specs=P(None, "group", "wide"), check_vma=False
    )
```

```python
import functools
import math

import jax
import jax.numpy as jnp
import numpy as np
from jax import lax
from jax.experimental import pallas as pl
from jax.experimental.pallas import tpu as pltpu
from jax.sharding import PartitionSpec as P

SUB = 32
HALF = SUB // 2
VIS = 128
GRID = 4096
TILES = GRID // SUB
F32 = jnp.float32
BF16 = jnp.bfloat16


def _poly_coefs(most, degree):
    top = most**2
    nodes = top / 2 * (1 + np.cos(np.pi * (np.arange(64) + 0.5) / 64))
    r = np.sqrt(nodes)
    cheb = np.polynomial.chebyshev.Chebyshev
    c = cheb.fit(nodes, np.cos(2 * np.pi * r), degree, domain=[0, top])
    s = cheb.fit(nodes, np.sin(2 * np.pi * r) / r, degree, domain=[0, top])
    poly = np.polynomial.Polynomial
    return (
        [float(v) for v in c.convert(kind=poly).coef],
        [float(v) for v in s.convert(kind=poly).coef],
    )


ANY_TURN = _poly_coefs(0.5, 5)
SMALL_TURN = _poly_coefs((SUB / 2 - 2) / (2 * SUB), 4)


def cis(r, coefs):
    z = r * r
    c, s = coefs[0][-1], coefs[1][-1]
    for k in range(len(coefs[0]) - 2, -1, -1):
        c = c * z + coefs[0][k]
        s = s * z + coefs[1][k]
    return c, s * r


def cmul(a, b):
    return a[0] * b[0] - a[1] * b[1], a[0] * b[1] + a[1] * b[0]


def split(x):
    hi = x.astype(BF16)
    lo = (x - hi.astype(F32)).astype(BF16)
    return hi, lo


def np_tables():
    t = np.arange(SUB)
    q = np.arange(SUB)
    n0 = np.arange(TILES)
    g = np.einsum(
        "tq,qn->tn",
        np.exp(-2j * np.pi * np.outer(t, q) / SUB),
        np.exp(-2j * np.pi * np.outer(q, n0) / GRID),
    )
    w = np.exp(-2j * np.pi * (np.outer(n0, n0) % TILES) / TILES)
    return g, w


def to_waves(g):
    sign = (-1.0) ** np.arange(HALF)[None, :, None]
    up = g[:, HALF:] * sign
    down = g[:, HALF - 1 :: -1] * -sign
    return np.concatenate([up + down, 1j * (up - down)], 1)


def shifted(g):
    index = (np.arange(SUB)[:, None] + np.arange(SUB)[None, :]) % SUB
    return to_waves(g[index])


def pixel_rows(raw_ref, size, out_ref, row_ref, wave_ref):
    lane = lax.broadcasted_iota(jnp.int32, (SUB, VIS), 1)
    step = (lax.broadcasted_iota(jnp.int32, (8, VIS), 0).astype(F32) + 0.5) / SUB
    cat = jnp.concatenate

    def prepare(t):
        ar, ai, u, v = (raw_ref[q * size + t * 8 : q * size + t * 8 + 8] for q in range(4))
        first_u, first_v = (cis((x - HALF) * (1.0 / (2 * SUB)), SMALL_TURN) for x in (u, v))
        twice = cmul(first_u, first_u)
        wave = first_u
        for m in range(8):
            if m:
                wave = cmul(wave, twice)
            for part in range(2):
                row = t * 8 * 16 + part * 8 + m
                wave_ref[pl.ds(row, 8, stride=16), :] = wave[part]
        step_u = cmul(wave, first_u)
        step_v = first_v
        for _ in range(4):
            step_v = cmul(step_v, step_v)
        pr, pi = cmul(first_u, first_v)
        rows = [*step_u, *step_v, ar * pr + ai * pi, ai * pr - ar * pi, v - HALF]
        for q, row in enumerate(rows):
            row_ref[t, q] = row

    def parts(n):
        t, d = n // 8, n % 8
        bc = lambda q: jnp.broadcast_to(row_ref[t, q, d : d + 1, :], (8, VIS))
        ur, ui, vr, vi, ar, ai, v = (bc(q) for q in range(7))
        cu, su = (wave_ref[n * 16 + q * 8 : n * 16 + q * 8 + 8] for q in range(2))
        turns = v * step
        cv, sv = cis(turns - jnp.round(turns), ANY_TURN)
        ahead = lambda c, s, r, i: [c, c * r - s * i, s, c * i + s * r]
        us = ahead(cu, su, ur, ui)
        vs = ahead(cv, sv, vr, vi)
        wh, wl = split(cat([ar * x for x in us] + [ai * x for x in us], 0))
        vh, vl = split(cat(vs, 0))
        return cat([wh, wl], 1), cat([vh, vh], 1), cat([vl, vl], 1)

    def pair(n):
        one, two = parts(n), parts(n + 1)
        prod = lax.dot_general(
            cat([one[0], two[0]], 0),
            cat([one[1], two[1], one[2], two[2]], 0),
            (((1,), (1,)), ((), ())),
            preferred_element_type=F32,
        )
        ar, ai, br, bi = (prod[q * SUB : q * SUB + SUB] for q in range(4))
        fold = lambda p, q, r, s: jnp.where(
            lane < 64, jnp.where(lane < 32, p, q), jnp.where(lane < 96, r, s)
        )
        out_ref[n // 2] = fold(ar, bi, ai, br) + pltpu.roll(fold(ai, br, ar, bi), 64, 1)

    prepare(0)
    for t in range(size // 8):
        if t + 1 < size // 8:
            prepare(t + 1)
        for d in range(0, 8, 2):
            pair(t * 8 + d)


def gather_kernel(
    wide, subs, size, band, count_ref, owner_ref, row_in_ref, col_ref, vis_ref, off_ref,
    pix_hbm, ids_hbm,
    raw_ref, row_ref, wave_ref, out_ref,
    send_sem, recv_sem, loc_sem, pix_send, pix_recv, id_loc, id_send, id_recv,
):
    depth = wide // 4
    pieces = subs // size
    trips = 2 * depth * pieces
    relays = (depth - 1) * pieces
    me = lax.axis_index("wide")
    core, y, z = me % 2, (me // 2) % 2, me // 4
    place = lambda zz, yy, cc: (zz * 2 + yy) * 2 + cc
    partner = {"wide": place(z, y, 1 - core)}
    across = {"wide": place(z, 1 - y, core)}
    above = {"wide": place(jnp.minimum(z + 1, depth - 1), y, core)}
    below = {"wide": place(jnp.maximum(z - 1, 0), y, core)}
    not_top, not_bottom = z < depth - 1, z > 0
    mesh_id = pl.DeviceIdType.MESH
    here = z * 2 + y

    barrier = pltpu.get_barrier_semaphore()
    for peer in (partner, across):
        pl.semaphore_signal(barrier, inc=1, device_id=peer, device_id_type=mesh_id)

    @pl.when(not_top)
    def _():
        pl.semaphore_signal(barrier, inc=1, device_id=above, device_id_type=mesh_id)

    @pl.when(not_bottom)
    def _():
        pl.semaphore_signal(barrier, inc=1, device_id=below, device_id_type=mesh_id)

    slots = lax.broadcasted_iota(jnp.int32, (8, VIS), 1)
    for piece in range(pieces):

        def stage(t, ids):
            for d in range(8):
                j = t * 8 + d
                n = piece * size + j
                live = jnp.where(slots[:2] < count_ref[n], 1.0 / math.sqrt(VIS), 0.0)
                for half, pair in enumerate((vis_ref[n] * live, off_ref[n])):
                    for q in range(2):
                        raw_ref[here, piece, pl.ds((half * 2 + q) * size + j, 1), :] = pair[q : q + 1]
                tile = (owner_ref[n] * band + row_in_ref[n]) * TILES + col_ref[n]
                ids = jnp.where(slots == j, tile, ids)
            return ids

        ids = lax.fori_loop(0, size // 8, stage, jnp.zeros((8, VIS), jnp.int32))
        raw_ref[here, piece, 4 * size :, :] = ids.astype(F32)
    neighbours = jnp.minimum(z, 1) + jnp.minimum(depth - 1 - z, 1)
    pl.semaphore_wait(barrier, 2 + neighbours)

    def hop(zz, yy, piece, to, way):
        chip = zz * 2 + yy
        return pltpu.make_async_remote_copy(
            src_ref=raw_ref.at[chip, piece],
            dst_ref=raw_ref.at[chip, piece],
            send_sem=send_sem.at[zz, piece, way],
            recv_sem=recv_sem.at[chip, piece],
            device_id=to,
            device_id_type=mesh_id,
        )

    def spread_out(zz, piece, act):
        act(hop(zz, y, piece, across, 2))

        @pl.when((zz <= z) & not_top)
        def _():
            act(hop(zz, y, piece, above, 0))

        @pl.when((zz >= z) & not_bottom)
        def _():
            act(hop(zz, y, piece, below, 1))

    for piece in range(pieces):
        spread_out(z, piece, lambda copy: copy.start())

    def pass_on(number):
        far, piece = number // pieces + 1, number % pieces
        for zz, inside in ((z - far, z - far >= 0), (z + far, z + far < depth)):

            @pl.when(inside)
            def _():
                hop(zz, y, piece, across, 2).wait_recv()
                spread_out(zz, piece, lambda copy: copy.start())

    near = jnp.minimum(z, depth - 1 - z)

    def order(k):
        swing = z + ((k + 1) // 2) * (1 - 2 * (k % 2))
        edge = jnp.where(z * 2 < depth - 1, k, depth - 1 - k)
        return jnp.where(k <= 2 * near, swing, edge)

    def copies(number, chip, piece):
        rows = pl.ds(((chip * 2 + core) * subs + piece * size) // 2, size // 2)
        slot = number % 2
        mine = pltpu.make_async_copy(out_ref.at[slot], pix_hbm.at[rows], loc_sem.at[slot])
        theirs = pltpu.make_async_remote_copy(
            src_ref=out_ref.at[slot],
            dst_ref=pix_hbm.at[rows],
            send_sem=pix_send.at[slot],
            recv_sem=pix_recv.at[number],
            device_id=partner,
            device_id_type=mesh_id,
        )
        return mine, theirs

    def id_copies(number, chip, piece):
        block = raw_ref.at[chip, piece, pl.ds(4 * size, 8)]
        where = ids_hbm.at[(chip * 2 + core) * pieces + piece]
        mine = pltpu.make_async_copy(block, where, id_loc.at[number])
        theirs = pltpu.make_async_remote_copy(
            src_ref=block,
            dst_ref=where,
            send_sem=id_send.at[number],
            recv_sem=id_recv.at[number],
            device_id=partner,
            device_id_type=mesh_id,
        )
        return mine, theirs

    def body(number, carry):
        later = number - pieces
        end = later - 2 * relays
        other = jnp.where(later >= 0, jnp.where(end >= 0, 1, 1 - later % 2), 0)
        at_turn = jnp.where(later >= 0, jnp.where(end >= 0, relays + end, later // 2), number)
        relayed = jnp.where(later >= 0, 1 - other, 0)
        relay = at_turn - pieces * (1 - relayed)
        first = relay < 0
        paired = relay < 2 * near * pieces
        group = 2 * pieces
        k = jnp.where(paired, 1 + relay // group * 2 + relay % 2, 1 + relay // pieces)
        k = jnp.where(first, 0, k)
        piece = jnp.where(paired, relay % group // 2, relay % pieces)
        piece = jnp.where(first, at_turn, piece)
        zz = order(k)
        yy = y + other * (1 - 2 * y)
        chip = zz * 2 + yy

        @pl.when(other == 1)
        def _():
            hop(zz, yy, piece, across, 2).wait_recv()

        for copy in id_copies(number, chip, piece):
            copy.start()

        @pl.when(number >= 2)
        def _():
            mine, theirs = copies(number, chip, piece)
            mine.wait()
            theirs.wait_send()

        pixel_rows(raw_ref.at[chip, piece], size, out_ref.at[number % 2], row_ref, wave_ref)
        for copy in copies(number, chip, piece):
            copy.start()

        @pl.when((number % 2 == 1) & (number // 2 < relays))
        def _():
            pass_on(number // 2)

        return carry

    lax.fori_loop(0, trips, body, 0)

    def drain(number, carry):
        spread_out(number // pieces, number % pieces, lambda copy: copy.wait_send())
        return carry

    lax.fori_loop(0, depth * pieces, drain, 0)
    for number in range(2):
        mine, theirs = copies(number, here, 0)
        mine.wait()
        theirs.wait_send()

    def arrive(number, carry):
        mine, theirs = id_copies(number, here, 0)
        mine.wait()
        theirs.wait()
        copies(number, here, 0)[1].wait_recv()
        return carry

    lax.fori_loop(0, trips, arrive, 0)


def gather(scalars, visibilities, offsets, wide, size, band):
    subs = visibilities.shape[0]
    depth = wide // 4
    pieces = subs // size
    trips = 2 * depth * pieces
    dma = pltpu.SemaphoreType.DMA
    anywhere = pl.BlockSpec(memory_space=pl.ANY)
    whole = pl.BlockSpec(memory_space=pltpu.VMEM)
    return pl.pallas_call(
        functools.partial(gather_kernel, wide, subs, size, band),
        out_shape=[
            jax.ShapeDtypeStruct((wide * subs // 2, SUB, 128), F32),
            jax.ShapeDtypeStruct((wide * pieces, 8, 128), F32),
        ],
        in_specs=[pl.BlockSpec(memory_space=pltpu.SMEM)] * 4 + [whole, whole],
        out_specs=[anywhere, anywhere],
        scratch_shapes=[
            pltpu.VMEM((wide // 2, pieces, 4 * size + 8, 128), F32),
            pltpu.VMEM((size // 8, 7, 8, VIS), F32),
            pltpu.VMEM((size * 16, VIS), F32),
            pltpu.VMEM((2, size // 2, SUB, 128), F32),
            dma((depth, pieces, 3)),
            dma((wide // 2, pieces)),
            dma((2,)),
            dma((2,)),
            dma((trips,)),
            dma((trips,)),
            dma((trips,)),
            dma((trips,)),
        ],
        compiler_params=pltpu.CompilerParams(collective_id=0, has_side_effects=True),
        name="gather",
    )(*scalars, visibilities, offsets)


def fft(xs):
    n = len(xs)
    if n == 1:
        return xs
    even, odd = fft(xs[::2]), fft(xs[1::2])
    low, high = [], []
    root = math.sqrt(0.5)
    for k, ((er, ei), (r, i)) in enumerate(zip(even, odd)):
        if k == 0:
            tr, ti = r, i
        elif 4 * k == n:
            low.append((er + i, ei - r))
            high.append((er - i, ei + r))
            continue
        elif 8 * k == n:
            tr, ti = (r + i) * root, (i - r) * root
        elif 8 * k == 3 * n:
            tr, ti = (i - r) * root, (r + i) * -root
        else:
            tr, ti = turn(r, i, k / n)
        low.append((er + tr, ei + ti))
        high.append((er - tr, ei - ti))
    return low + high


def turn(r, i, turns):
    c, s = math.cos(2 * math.pi * turns), math.sin(2 * math.pi * turns)
    return r * c + i * s, i * c - r * s


def finish_kernel(
    block, size, nc, shift, p_ref, ids_ref, phr_ref, phi_ref, waves_hbm, mix_hbm, out_hbm,
    x_ref, b_ref, y_ref, tab_ref, wave_ref, mix_ref, idv_ref, ids_smem, sem, id_sem, mix_sem, out_sem,
):
    g = pl.program_id(0)
    steps = pl.num_programs(0)
    halves = nc // 128
    chunk = 16
    rows = chunk * 16

    @pl.when(g == 0)
    def _():
        first = lax.axis_index("wide") * halves
        pltpu.make_async_copy(mix_hbm, mix_ref, mix_sem).start()
        load = pltpu.make_async_copy(waves_hbm.at[pl.ds(first, halves)], wave_ref, sem)
        load.start()

        def number(t, carry):
            idv_ref[pl.ds(t, 1), :] = ids_ref[t, 0:1, :].astype(jnp.int32)
            return carry

        lax.fori_loop(0, ids_ref.shape[0], number, 0, unroll=4)
        scalars = pltpu.make_async_copy(idv_ref, ids_smem, id_sem)
        scalars.start()

        def zero(t, carry):
            for lt in range(2 * halves):
                for ref in (b_ref, x_ref):
                    ref[lt, pl.ds(t * 32, 32), :] = jnp.zeros((32, 128), F32)
            return carry

        lax.fori_loop(0, TILES, zero, 0)
        load.wait()
        tab_ref[...] = jnp.zeros(tab_ref.shape, BF16)
        for n in range(halves):
            left = slice(n * 128, n * 128 + 128)
            right = slice(nc + n * 128, nc + n * 128 + 128)
            for row, low in ((0, 0), (32, 0), (128, 64)):
                dr = wave_ref[n, low : low + 32]
                di = wave_ref[n, low + 32 : low + 64]
                tab_ref[row : row + 32, left] = dr
                tab_ref[row : row + 32, right] = di
                tab_ref[row + 64 : row + 96, left] = -di
                tab_ref[row + 64 : row + 96, right] = dr
        scalars.wait()

    early = lax.broadcasted_iota(jnp.int32, (rows, 128), 1) % 64 < 32

    def multiply(t, slot):
        p = p_ref[pl.ds(t * chunk // 2, chunk // 2)].reshape(rows, 128)
        hi = p.astype(BF16)
        hif = hi.astype(F32)
        lof = p - hif
        lo = lof.astype(BF16)
        hir = pltpu.roll(hi, 32, 1)
        one = jnp.where(early, hi, pltpu.roll(lo, 32, 1))
        two = jnp.where(early, hir, pltpu.roll(lo, 64, 1))
        lhs = jnp.concatenate(
            [
                jnp.concatenate([one, hi], 1),
                jnp.concatenate([two, hir], 1),
            ],
            0,
        )
        y_ref[slot] = jnp.dot(lhs, tab_ref[...], preferred_element_type=F32)

    def add(t, slot):
        for d in range(chunk):
            at = t * chunk + d
            tile = ids_smem[g * (block // size) + at // size, at % size]
            r = lax.shift_right_logical(tile, shift)
            c = lax.bitwise_and(tile, TILES - 1)
            pr = jnp.broadcast_to(phr_ref[pl.ds(c, 1), :], (8, 128))
            pi = jnp.broadcast_to(phi_ref[pl.ds(c, 1), :], (8, 128))
            dst = pl.ds(pl.multiple_of(r * 32, 32), 32)
            acc = b_ref if d % 2 else x_ref
            old = acc[:, dst, :]
            y = y_ref[slot, pl.ds(d % 2 * rows + d // 2 * SUB, SUB), :]
            real, imag = [], []
            for n in range(halves):
                yr = y[:, n * 128 : n * 128 + 128].reshape(4, 8, 128)
                yi = y[:, nc + n * 128 : nc + n * 128 + 128].reshape(4, 8, 128)
                real.append((yr * pr - yi * pi).reshape(1, 32, 128))
                imag.append((yr * pi + yi * pr).reshape(1, 32, 128))
            acc[:, dst, :] = old + jnp.concatenate(real + imag, 0)

    trips = block // chunk
    multiply(0, 0)
    for t in range(trips):
        if t + 1 < trips:
            multiply(t + 1, (t + 1) % 2)
        add(t, t % 2)

    @pl.when(g == steps - 1)
    def _():
        at = lambda r, it: pl.ds(pl.multiple_of(r * 32 + it * 8, 8), 8)

        def eights(t, carry):
            n, it = t // 4, t % 4
            for b in range(16):
                xs = []
                for a in range(8):
                    pick = at(16 * a + b, it)
                    xs.append(
                        tuple(
                            x_ref[o * halves + n, pick, :] + b_ref[o * halves + n, pick, :]
                            for o in range(2)
                        )
                    )
                for k, (r, i) in enumerate(fft(xs)):
                    if b * k:
                        r, i = turn(r, i, b * k / TILES)
                    pick = at(16 * k + b, it)
                    x_ref[n, pick, :] = r
                    x_ref[halves + n, pick, :] = i
            return carry

        def sixteens(t, carry):
            n, it = t // 4, t % 4
            for a in range(8):
                xs = []
                for b in range(16):
                    pick = at(16 * a + b, it)
                    xs.append((x_ref[n, pick, :], x_ref[halves + n, pick, :]))
                for k, (r, i) in enumerate(fft(xs)):
                    pick = at(a + 8 * k, it)
                    b_ref[n, pick, :] = r
                    b_ref[halves + n, pick, :] = i
            return carry

        def mix(n, t, carry):
            parts = []
            for d in range(8):
                m = t * 8 + d
                near = pl.ds(pl.multiple_of(m * SUB, SUB), SUB)
                zh, zl = split(
                    jnp.concatenate([b_ref[o * halves + n, near, :] for o in range(2)], 0)
                )
                both = mix_ref[m]
                res = jnp.dot(
                    jnp.concatenate([both, both[:, :64]], 1),
                    jnp.concatenate([zh, zh, zl], 0),
                    preferred_element_type=F32,
                )
                parts.append(res[None])
            for q in range(8):
                block8 = jnp.concatenate([p[:, q * 8 : q * 8 + 8] for p in parts], 0)
                turned = jnp.transpose(block8, (1, 0, 2))
                for e in range(8):
                    p, b = divmod(q * 8 + e, SUB)
                    far = pl.ds(pl.multiple_of(b * TILES + t * 8, 8), 8)
                    x_ref[p * halves + n, far, :] = turned[e]
            return carry

        stores = []
        for n in range(halves):
            lax.fori_loop(4 * n, 4 * n + 4, eights, 0)
            lax.fori_loop(4 * n, 4 * n + 4, sixteens, 0)
            if n == 0:
                pltpu.make_async_copy(mix_hbm, mix_ref, mix_sem).wait()
            lax.fori_loop(0, TILES // 8, functools.partial(mix, n), 0)
            for p in range(2):
                store = pltpu.make_async_copy(
                    x_ref.at[p * halves + n],
                    out_hbm.at[p, :, pl.ds(n * 128, 128)],
                    out_sem.at[p * halves + n],
                )
                store.start()
                stores.append(store)
        for store in stores:
            store.wait()


def finish(pix, ids, phr, phi, waves, mix, nc, size):
    count = pix.shape[0] * 2
    block = math.gcd(count, 2 * size)
    tiles = 2 * nc // 128
    const = lambda shape: pl.BlockSpec(shape, lambda g: (0,) * len(shape))
    anywhere = pl.BlockSpec(memory_space=pl.ANY)
    x_shape = (tiles, GRID, 128)
    dma = pltpu.SemaphoreType.DMA
    return pl.pallas_call(
        functools.partial(finish_kernel, block, size, nc, TILES.bit_length() - 1),
        out_shape=jax.ShapeDtypeStruct((2, GRID, nc), F32),
        grid=(count // block,),
        in_specs=[
            pl.BlockSpec((block // 2, SUB, 128), lambda g: (g, 0, 0)),
            const(ids.shape),
            const(phr.shape),
            const(phi.shape),
            anywhere,
            anywhere,
        ],
        out_specs=anywhere,
        scratch_shapes=[
            pltpu.VMEM(x_shape, F32),
            pltpu.VMEM(x_shape, F32),
            pltpu.VMEM((2, 512, 2 * nc), F32),
            pltpu.VMEM((256, 2 * nc), BF16),
            pltpu.VMEM((nc // 128, 128, 128), BF16),
            pltpu.VMEM(mix.shape, BF16),
            pltpu.VMEM((count // size, 128), jnp.int32),
            pltpu.SMEM((count // size, 128), jnp.int32),
            dma,
            dma,
            dma,
            dma((tiles,)),
        ],
        name="finish",
    )(pix, ids, phr, phi, waves, mix)


def np_split(x):
    hi = x.astype(np.float32).astype(BF16)
    return hi, (x - hi.astype(np.float64)).astype(BF16)


def column_waves(g):
    waves = shifted(g) / 512.0
    rh, rl = np_split(waves.real)
    ih, il = np_split(waves.imag)
    return np.concatenate([rh, ih, rl, il], 1)


def real_form(z):
    return np.array([[z.real, -z.imag], [z.imag, z.real]])


def per_device(visibilities, offsets, vis_count, owner, tile_row, tile_col):
    wide = lax.axis_size("wide")
    nc = GRID // wide
    band = GRID // (SUB * wide)
    g, w = np_tables()
    subs = visibilities.shape[0]
    size = math.gcd(subs, 96)
    scalars = (vis_count, owner, tile_row, tile_col)
    pix, ids = gather(scalars, visibilities, offsets, wide, size, band)
    m4 = real_form(shifted(g) / 256.0).transpose(4, 0, 2, 1, 3).reshape(TILES, 64, 64)
    both = jnp.asarray(np.concatenate(np_split(m4), 2))
    phr, phi = jnp.asarray(w.real, F32), jnp.asarray(w.imag, F32)
    return finish(pix, ids, phr, phi, jnp.asarray(column_waves(g)), both, nc, size)


def solution(mesh):
    placed = (
        P(("group", "wide"), None, None),
        P(("group", "wide"), None, None),
        P(("group", "wide")),
        P(("group", "wide")),
        P(("group", "wide")),
        P(("group", "wide")),
    )
    return jax.shard_map(
        per_device, mesh=mesh, in_specs=placed, out_specs=P(None, "group", "wide"), check_vma=False
    )
```

```python
import functools
import math

import jax
import jax.numpy as jnp
import numpy as np
from jax import lax
from jax.experimental import pallas as pl
from jax.experimental.pallas import tpu as pltpu
from jax.sharding import PartitionSpec as P

SUB = 32
HALF = SUB // 2
VIS = 128
GRID = 4096
TILES = GRID // SUB
F32 = jnp.float32
BF16 = jnp.bfloat16


def _poly_coefs(most, degree):
    top = most**2
    nodes = top / 2 * (1 + np.cos(np.pi * (np.arange(64) + 0.5) / 64))
    r = np.sqrt(nodes)
    cheb = np.polynomial.chebyshev.Chebyshev
    c = cheb.fit(nodes, np.cos(2 * np.pi * r), degree, domain=[0, top])
    s = cheb.fit(nodes, np.sin(2 * np.pi * r) / r, degree, domain=[0, top])
    poly = np.polynomial.Polynomial
    return (
        [float(v) for v in c.convert(kind=poly).coef],
        [float(v) for v in s.convert(kind=poly).coef],
    )


ANY_TURN = _poly_coefs(0.5, 5)
SMALL_TURN = _poly_coefs((SUB / 2 - 2) / (2 * SUB), 4)


def cis(r, coefs):
    z = r * r
    c, s = coefs[0][-1], coefs[1][-1]
    for k in range(len(coefs[0]) - 2, -1, -1):
        c = c * z + coefs[0][k]
        s = s * z + coefs[1][k]
    return c, s * r


def cmul(a, b):
    return a[0] * b[0] - a[1] * b[1], a[0] * b[1] + a[1] * b[0]


def split(x):
    hi = x.astype(BF16)
    lo = (x - hi.astype(F32)).astype(BF16)
    return hi, lo


def np_tables():
    t = np.arange(SUB)
    q = np.arange(SUB)
    n0 = np.arange(TILES)
    g = np.einsum(
        "tq,qn->tn",
        np.exp(-2j * np.pi * np.outer(t, q) / SUB),
        np.exp(-2j * np.pi * np.outer(q, n0) / GRID),
    )
    w = np.exp(-2j * np.pi * (np.outer(n0, n0) % TILES) / TILES)
    return g, w


def to_waves(g):
    sign = (-1.0) ** np.arange(HALF)[None, :, None]
    up = g[:, HALF:] * sign
    down = g[:, HALF - 1 :: -1] * -sign
    return np.concatenate([up + down, 1j * (up - down)], 1)


def shifted(g):
    index = (np.arange(SUB)[:, None] + np.arange(SUB)[None, :]) % SUB
    return to_waves(g[index])


def pixel_rows(raw_ref, size, out_ref, row_ref, wave_ref):
    lane = lax.broadcasted_iota(jnp.int32, (SUB, VIS), 1)
    step = (lax.broadcasted_iota(jnp.int32, (8, VIS), 0).astype(F32) + 0.5) / SUB
    cat = jnp.concatenate

    def prepare(t):
        ar, ai, u, v = (raw_ref[q * size + t * 8 : q * size + t * 8 + 8] for q in range(4))
        first_u, first_v = (cis((x - HALF) * (1.0 / (2 * SUB)), SMALL_TURN) for x in (u, v))
        twice = cmul(first_u, first_u)
        wave = first_u
        for m in range(8):
            if m:
                wave = cmul(wave, twice)
            for part in range(2):
                row = t * 8 * 16 + part * 8 + m
                wave_ref[pl.ds(row, 8, stride=16), :] = wave[part]
        step_u = cmul(wave, first_u)
        step_v = first_v
        for _ in range(4):
            step_v = cmul(step_v, step_v)
        pr, pi = cmul(first_u, first_v)
        rows = [*step_u, *step_v, ar * pr + ai * pi, ai * pr - ar * pi, v - HALF]
        for q, row in enumerate(rows):
            row_ref[t, q] = row

    def parts(n):
        t, d = n // 8, n % 8
        bc = lambda q: jnp.broadcast_to(row_ref[t, q, d : d + 1, :], (8, VIS))
        ur, ui, vr, vi, ar, ai, v = (bc(q) for q in range(7))
        cu, su = (wave_ref[n * 16 + q * 8 : n * 16 + q * 8 + 8] for q in range(2))
        turns = v * step
        cv, sv = cis(turns - jnp.round(turns), ANY_TURN)
        ahead = lambda c, s, r, i: [c, c * r - s * i, s, c * i + s * r]
        us = ahead(cu, su, ur, ui)
        vs = ahead(cv, sv, vr, vi)
        wh, wl = split(cat([ar * x for x in us] + [ai * x for x in us], 0))
        vh, vl = split(cat(vs, 0))
        return cat([wh, wl], 1), cat([vh, vh], 1), cat([vl, vl], 1)

    def pair(n):
        one, two = parts(n), parts(n + 1)
        prod = lax.dot_general(
            cat([one[0], two[0]], 0),
            cat([one[1], two[1], one[2], two[2]], 0),
            (((1,), (1,)), ((), ())),
            preferred_element_type=F32,
        )
        ar, ai, br, bi = (prod[q * SUB : q * SUB + SUB] for q in range(4))
        fold = lambda p, q, r, s: jnp.where(
            lane < 64, jnp.where(lane < 32, p, q), jnp.where(lane < 96, r, s)
        )
        out_ref[n // 2] = fold(ar, bi, ai, br) + pltpu.roll(fold(ai, br, ar, bi), 64, 1)

    prepare(0)
    for t in range(size // 8):
        if t + 1 < size // 8:
            prepare(t + 1)
        for d in range(0, 8, 2):
            pair(t * 8 + d)


def gather_kernel(
    wide, subs, size, band, count_ref, owner_ref, row_in_ref, col_ref, vis_ref, off_ref,
    pix_hbm, ids_hbm,
    raw_ref, row_ref, wave_ref, out_ref,
    send_sem, recv_sem, loc_sem, pix_send, pix_recv, id_loc, id_send, id_recv,
):
    depth = wide // 4
    pieces = subs // size
    trips = 2 * depth * pieces
    relays = (depth - 1) * pieces
    me = lax.axis_index("wide")
    core, y, z = me % 2, (me // 2) % 2, me // 4
    place = lambda zz, yy, cc: (zz * 2 + yy) * 2 + cc
    partner = {"wide": place(z, y, 1 - core)}
    across = {"wide": place(z, 1 - y, core)}
    above = {"wide": place(jnp.minimum(z + 1, depth - 1), y, core)}
    below = {"wide": place(jnp.maximum(z - 1, 0), y, core)}
    not_top, not_bottom = z < depth - 1, z > 0
    mesh_id = pl.DeviceIdType.MESH
    here = z * 2 + y

    barrier = pltpu.get_barrier_semaphore()
    for peer in (partner, across):
        pl.semaphore_signal(barrier, inc=1, device_id=peer, device_id_type=mesh_id)

    @pl.when(not_top)
    def _():
        pl.semaphore_signal(barrier, inc=1, device_id=above, device_id_type=mesh_id)

    @pl.when(not_bottom)
    def _():
        pl.semaphore_signal(barrier, inc=1, device_id=below, device_id_type=mesh_id)

    slots = lax.broadcasted_iota(jnp.int32, (8, VIS), 1)
    def stage_piece(piece):
        def stage(t, ids):
            for d in range(8):
                j = t * 8 + d
                n = piece * size + j
                live = jnp.where(slots[:2] < count_ref[n], 1.0 / math.sqrt(VIS), 0.0)
                for half, pair in enumerate((vis_ref[n] * live, off_ref[n])):
                    for q in range(2):
                        raw_ref[here, piece, pl.ds((half * 2 + q) * size + j, 1), :] = pair[q : q + 1]
                tile = (owner_ref[n] * band + row_in_ref[n]) * TILES + col_ref[n]
                ids = jnp.where(slots == j, tile, ids)
            return ids

        ids = lax.fori_loop(0, size // 8, stage, jnp.zeros((8, VIS), jnp.int32))
        raw_ref[here, piece, 4 * size :, :] = ids.astype(F32)

    stage_piece(0)
    neighbours = jnp.minimum(z, 1) + jnp.minimum(depth - 1 - z, 1)
    pl.semaphore_wait(barrier, 2 + neighbours)

    def hop(zz, yy, piece, to, way):
        chip = zz * 2 + yy
        return pltpu.make_async_remote_copy(
            src_ref=raw_ref.at[chip, piece],
            dst_ref=raw_ref.at[chip, piece],
            send_sem=send_sem.at[zz, piece, way],
            recv_sem=recv_sem.at[chip, piece],
            device_id=to,
            device_id_type=mesh_id,
        )

    def spread_out(zz, piece, act):
        act(hop(zz, y, piece, across, 2))

        @pl.when((zz <= z) & not_top)
        def _():
            act(hop(zz, y, piece, above, 0))

        @pl.when((zz >= z) & not_bottom)
        def _():
            act(hop(zz, y, piece, below, 1))

    spread_out(z, 0, lambda copy: copy.start())
    for piece in range(1, pieces):
        stage_piece(piece)

    def pass_on(number):
        far, piece = number // pieces + 1, number % pieces
        for zz, inside in ((z - far, z - far >= 0), (z + far, z + far < depth)):

            @pl.when(inside)
            def _():
                hop(zz, y, piece, across, 2).wait_recv()
                spread_out(zz, piece, lambda copy: copy.start())

    near = jnp.minimum(z, depth - 1 - z)

    def order(k):
        swing = z + ((k + 1) // 2) * (1 - 2 * (k % 2))
        edge = jnp.where(z * 2 < depth - 1, k, depth - 1 - k)
        return jnp.where(k <= 2 * near, swing, edge)

    def copies(number, chip, piece):
        rows = pl.ds(((chip * 2 + core) * subs + piece * size) // 2, size // 2)
        slot = number % 2
        mine = pltpu.make_async_copy(out_ref.at[slot], pix_hbm.at[rows], loc_sem.at[slot])
        theirs = pltpu.make_async_remote_copy(
            src_ref=out_ref.at[slot],
            dst_ref=pix_hbm.at[rows],
            send_sem=pix_send.at[slot],
            recv_sem=pix_recv.at[number],
            device_id=partner,
            device_id_type=mesh_id,
        )
        return mine, theirs

    def id_copies(number, chip, piece):
        block = raw_ref.at[chip, piece, pl.ds(4 * size, 8)]
        where = ids_hbm.at[(chip * 2 + core) * pieces + piece]
        mine = pltpu.make_async_copy(block, where, id_loc.at[number])
        theirs = pltpu.make_async_remote_copy(
            src_ref=block,
            dst_ref=where,
            send_sem=id_send.at[number],
            recv_sem=id_recv.at[number],
            device_id=partner,
            device_id_type=mesh_id,
        )
        return mine, theirs

    def body(number, carry):
        later = number - pieces
        end = later - 2 * relays
        other = jnp.where(later >= 0, jnp.where(end >= 0, 1, 1 - later % 2), 0)
        at_turn = jnp.where(later >= 0, jnp.where(end >= 0, relays + end, later // 2), number)
        relayed = jnp.where(later >= 0, 1 - other, 0)
        relay = at_turn - pieces * (1 - relayed)
        first = relay < 0
        paired = relay < 2 * near * pieces
        group = 2 * pieces
        k = jnp.where(paired, 1 + relay // group * 2 + relay % 2, 1 + relay // pieces)
        k = jnp.where(first, 0, k)
        piece = jnp.where(paired, relay % group // 2, relay % pieces)
        piece = jnp.where(first, at_turn, piece)
        zz = order(k)
        yy = y + other * (1 - 2 * y)
        chip = zz * 2 + yy

        @pl.when(other == 1)
        def _():
            hop(zz, yy, piece, across, 2).wait_recv()

        for copy in id_copies(number, chip, piece):
            copy.start()

        @pl.when(number >= 2)
        def _():
            mine, theirs = copies(number, chip, piece)
            mine.wait()
            theirs.wait_send()

        pixel_rows(raw_ref.at[chip, piece], size, out_ref.at[number % 2], row_ref, wave_ref)
        for copy in copies(number, chip, piece):
            copy.start()

        @pl.when(number + 1 < pieces)
        def _():
            spread_out(z, number + 1, lambda copy: copy.start())

        @pl.when((number % 2 == 1) & (number // 2 < relays))
        def _():
            pass_on(number // 2)

        return carry

    lax.fori_loop(0, trips, body, 0)

    def drain(number, carry):
        spread_out(number // pieces, number % pieces, lambda copy: copy.wait_send())
        return carry

    lax.fori_loop(0, depth * pieces, drain, 0)
    for number in range(2):
        mine, theirs = copies(number, here, 0)
        mine.wait()
        theirs.wait_send()

    def arrive(number, carry):
        mine, theirs = id_copies(number, here, 0)
        mine.wait()
        theirs.wait()
        copies(number, here, 0)[1].wait_recv()
        return carry

    lax.fori_loop(0, trips, arrive, 0)


def gather(scalars, visibilities, offsets, wide, size, band):
    subs = visibilities.shape[0]
    depth = wide // 4
    pieces = subs // size
    trips = 2 * depth * pieces
    dma = pltpu.SemaphoreType.DMA
    anywhere = pl.BlockSpec(memory_space=pl.ANY)
    whole = pl.BlockSpec(memory_space=pltpu.VMEM)
    return pl.pallas_call(
        functools.partial(gather_kernel, wide, subs, size, band),
        out_shape=[
            jax.ShapeDtypeStruct((wide * subs // 2, SUB, 128), F32),
            jax.ShapeDtypeStruct((wide * pieces, 8, 128), F32),
        ],
        in_specs=[pl.BlockSpec(memory_space=pltpu.SMEM)] * 4 + [whole, whole],
        out_specs=[anywhere, anywhere],
        scratch_shapes=[
            pltpu.VMEM((wide // 2, pieces, 4 * size + 8, 128), F32),
            pltpu.VMEM((size // 8, 7, 8, VIS), F32),
            pltpu.VMEM((size * 16, VIS), F32),
            pltpu.VMEM((2, size // 2, SUB, 128), F32),
            dma((depth, pieces, 3)),
            dma((wide // 2, pieces)),
            dma((2,)),
            dma((2,)),
            dma((trips,)),
            dma((trips,)),
            dma((trips,)),
            dma((trips,)),
        ],
        compiler_params=pltpu.CompilerParams(collective_id=0, has_side_effects=True),
        name="gather",
    )(*scalars, visibilities, offsets)


def fft(xs):
    n = len(xs)
    if n == 1:
        return xs
    even, odd = fft(xs[::2]), fft(xs[1::2])
    low, high = [], []
    root = math.sqrt(0.5)
    for k, ((er, ei), (r, i)) in enumerate(zip(even, odd)):
        if k == 0:
            tr, ti = r, i
        elif 4 * k == n:
            low.append((er + i, ei - r))
            high.append((er - i, ei + r))
            continue
        elif 8 * k == n:
            tr, ti = (r + i) * root, (i - r) * root
        elif 8 * k == 3 * n:
            tr, ti = (i - r) * root, (r + i) * -root
        else:
            tr, ti = turn(r, i, k / n)
        low.append((er + tr, ei + ti))
        high.append((er - tr, ei - ti))
    return low + high


def turn(r, i, turns):
    c, s = math.cos(2 * math.pi * turns), math.sin(2 * math.pi * turns)
    return r * c + i * s, i * c - r * s


def finish_kernel(
    block, size, nc, shift, p_ref, ids_ref, phr_ref, phi_ref, waves_hbm, mix_hbm, out_hbm,
    x_ref, b_ref, y_ref, tab_ref, wave_ref, mix_ref, idv_ref, ids_smem, sem, id_sem, mix_sem, out_sem,
):
    g = pl.program_id(0)
    steps = pl.num_programs(0)
    halves = nc // 128
    chunk = 16
    rows = chunk * 16

    @pl.when(g == 0)
    def _():
        first = lax.axis_index("wide") * halves
        pltpu.make_async_copy(mix_hbm, mix_ref, mix_sem).start()
        load = pltpu.make_async_copy(waves_hbm.at[pl.ds(first, halves)], wave_ref, sem)
        load.start()

        def number(t, carry):
            idv_ref[pl.ds(t, 1), :] = ids_ref[t, 0:1, :].astype(jnp.int32)
            return carry

        lax.fori_loop(0, ids_ref.shape[0], number, 0, unroll=4)
        scalars = pltpu.make_async_copy(idv_ref, ids_smem, id_sem)
        scalars.start()

        def zero(t, carry):
            for lt in range(2 * halves):
                for ref in (b_ref, x_ref):
                    ref[lt, pl.ds(t * 32, 32), :] = jnp.zeros((32, 128), F32)
            return carry

        lax.fori_loop(0, TILES, zero, 0)
        load.wait()
        tab_ref[...] = jnp.zeros(tab_ref.shape, BF16)
        for n in range(halves):
            left = slice(n * 128, n * 128 + 128)
            right = slice(nc + n * 128, nc + n * 128 + 128)
            for row, low in ((0, 0), (32, 0), (128, 64)):
                dr = wave_ref[n, low : low + 32]
                di = wave_ref[n, low + 32 : low + 64]
                tab_ref[row : row + 32, left] = dr
                tab_ref[row : row + 32, right] = di
                tab_ref[row + 64 : row + 96, left] = -di
                tab_ref[row + 64 : row + 96, right] = dr
        scalars.wait()

    early = lax.broadcasted_iota(jnp.int32, (rows, 128), 1) % 64 < 32

    def multiply(t, slot):
        p = p_ref[pl.ds(t * chunk // 2, chunk // 2)].reshape(rows, 128)
        hi = p.astype(BF16)
        hif = hi.astype(F32)
        lof = p - hif
        lo = lof.astype(BF16)
        hir = pltpu.roll(hi, 32, 1)
        one = jnp.where(early, hi, pltpu.roll(lo, 32, 1))
        two = jnp.where(early, hir, pltpu.roll(lo, 64, 1))
        lhs = jnp.concatenate(
            [
                jnp.concatenate([one, hi], 1),
                jnp.concatenate([two, hir], 1),
            ],
            0,
        )
        y_ref[slot] = jnp.dot(lhs, tab_ref[...], preferred_element_type=F32)

    def add(t, slot):
        for d in range(chunk):
            at = t * chunk + d
            tile = ids_smem[g * (block // size) + at // size, at % size]
            r = lax.shift_right_logical(tile, shift)
            c = lax.bitwise_and(tile, TILES - 1)
            pr = jnp.broadcast_to(phr_ref[pl.ds(c, 1), :], (8, 128))
            pi = jnp.broadcast_to(phi_ref[pl.ds(c, 1), :], (8, 128))
            dst = pl.ds(pl.multiple_of(r * 32, 32), 32)
            acc = b_ref if d % 2 else x_ref
            old = acc[:, dst, :]
            y = y_ref[slot, pl.ds(d % 2 * rows + d // 2 * SUB, SUB), :]
            real, imag = [], []
            for n in range(halves):
                yr = y[:, n * 128 : n * 128 + 128].reshape(4, 8, 128)
                yi = y[:, nc + n * 128 : nc + n * 128 + 128].reshape(4, 8, 128)
                real.append((yr * pr - yi * pi).reshape(1, 32, 128))
                imag.append((yr * pi + yi * pr).reshape(1, 32, 128))
            acc[:, dst, :] = old + jnp.concatenate(real + imag, 0)

    trips = block // chunk
    multiply(0, 0)
    for t in range(trips):
        if t + 1 < trips:
            multiply(t + 1, (t + 1) % 2)
        add(t, t % 2)

    @pl.when(g == steps - 1)
    def _():
        at = lambda r, it: pl.ds(pl.multiple_of(r * 32 + it * 8, 8), 8)

        def eights(t, carry):
            n, it = t // 4, t % 4
            for b in range(16):
                xs = []
                for a in range(8):
                    pick = at(16 * a + b, it)
                    xs.append(
                        tuple(
                            x_ref[o * halves + n, pick, :] + b_ref[o * halves + n, pick, :]
                            for o in range(2)
                        )
                    )
                for k, (r, i) in enumerate(fft(xs)):
                    if b * k:
                        r, i = turn(r, i, b * k / TILES)
                    pick = at(16 * k + b, it)
                    x_ref[n, pick, :] = r
                    x_ref[halves + n, pick, :] = i
            return carry

        def sixteens(t, carry):
            n, it = t // 4, t % 4
            for a in range(8):
                xs = []
                for b in range(16):
                    pick = at(16 * a + b, it)
                    xs.append((x_ref[n, pick, :], x_ref[halves + n, pick, :]))
                for k, (r, i) in enumerate(fft(xs)):
                    pick = at(a + 8 * k, it)
                    b_ref[n, pick, :] = r
                    b_ref[halves + n, pick, :] = i
            return carry

        def mix(t, carry):
            parts = []
            for d in range(8):
                m = t * 8 + d
                near = pl.ds(pl.multiple_of(m * SUB, SUB), SUB)
                zm = jnp.concatenate(
                    [
                        jnp.concatenate([b_ref[o * halves + n, near, :] for n in range(halves)], 1)
                        for o in range(2)
                    ],
                    0,
                )
                zh, zl = split(zm)
                both = mix_ref[m]
                res = jnp.dot(
                    jnp.concatenate([both, both[:, :64]], 1),
                    jnp.concatenate([zh, zh, zl], 0),
                    preferred_element_type=F32,
                )
                parts.append(res[None])
            for n in range(halves):
                for q in range(8):
                    block8 = jnp.concatenate(
                        [p[:, q * 8 : q * 8 + 8, n * 128 : n * 128 + 128] for p in parts], 0
                    )
                    turned = jnp.transpose(block8, (1, 0, 2))
                    for e in range(8):
                        p, b = divmod(q * 8 + e, SUB)
                        far = pl.ds(pl.multiple_of(b * TILES + t * 8, 8), 8)
                        x_ref[p * halves + n, far, :] = turned[e]
            rows8 = pl.ds(pl.multiple_of(t * 8, 8), 8)
            for p in range(2):
                for n in range(halves):
                    pltpu.make_async_copy(
                        x_ref.reshape(2 * halves, SUB, TILES, 128).at[p * halves + n, :, rows8],
                        out_hbm.reshape(2, SUB, TILES, nc).at[p, :, rows8, pl.ds(n * 128, 128)],
                        out_sem.at[p * halves + n],
                    ).start()
            return carry

        lax.fori_loop(0, 4 * halves, eights, 0)
        lax.fori_loop(0, 4 * halves, sixteens, 0)
        pltpu.make_async_copy(mix_hbm, mix_ref, mix_sem).wait()
        lax.fori_loop(0, TILES // 8, mix, 0)
        for p in range(2):
            for n in range(halves):
                pltpu.make_async_copy(
                    x_ref.at[p * halves + n],
                    out_hbm.at[p, :, pl.ds(n * 128, 128)],
                    out_sem.at[p * halves + n],
                ).wait()


def finish(pix, ids, phr, phi, waves, mix, nc, size):
    count = pix.shape[0] * 2
    block = math.gcd(count, 2 * size)
    tiles = 2 * nc // 128
    const = lambda shape: pl.BlockSpec(shape, lambda g: (0,) * len(shape))
    anywhere = pl.BlockSpec(memory_space=pl.ANY)
    x_shape = (tiles, GRID, 128)
    dma = pltpu.SemaphoreType.DMA
    return pl.pallas_call(
        functools.partial(finish_kernel, block, size, nc, TILES.bit_length() - 1),
        out_shape=jax.ShapeDtypeStruct((2, GRID, nc), F32),
        grid=(count // block,),
        in_specs=[
            pl.BlockSpec((block // 2, SUB, 128), lambda g: (g, 0, 0)),
            const(ids.shape),
            const(phr.shape),
            const(phi.shape),
            anywhere,
            anywhere,
        ],
        out_specs=anywhere,
        scratch_shapes=[
            pltpu.VMEM(x_shape, F32),
            pltpu.VMEM(x_shape, F32),
            pltpu.VMEM((2, 512, 2 * nc), F32),
            pltpu.VMEM((256, 2 * nc), BF16),
            pltpu.VMEM((nc // 128, 128, 128), BF16),
            pltpu.VMEM(mix.shape, BF16),
            pltpu.VMEM((count // size, 128), jnp.int32),
            pltpu.SMEM((count // size, 128), jnp.int32),
            dma,
            dma,
            dma,
            dma((tiles,)),
        ],
        name="finish",
    )(pix, ids, phr, phi, waves, mix)


def np_split(x):
    hi = x.astype(np.float32).astype(BF16)
    return hi, (x - hi.astype(np.float64)).astype(BF16)


def column_waves(g):
    waves = shifted(g) / 512.0
    rh, rl = np_split(waves.real)
    ih, il = np_split(waves.imag)
    return np.concatenate([rh, ih, rl, il], 1)


def real_form(z):
    return np.array([[z.real, -z.imag], [z.imag, z.real]])


def per_device(visibilities, offsets, vis_count, owner, tile_row, tile_col):
    wide = lax.axis_size("wide")
    nc = GRID // wide
    band = GRID // (SUB * wide)
    g, w = np_tables()
    subs = visibilities.shape[0]
    size = math.gcd(subs, 96)
    scalars = (vis_count, owner, tile_row, tile_col)
    pix, ids = gather(scalars, visibilities, offsets, wide, size, band)
    m4 = real_form(shifted(g) / 256.0).transpose(4, 0, 2, 1, 3).reshape(TILES, 64, 64)
    both = jnp.asarray(np.concatenate(np_split(m4), 2))
    phr, phi = jnp.asarray(w.real, F32), jnp.asarray(w.imag, F32)
    return finish(pix, ids, phr, phi, jnp.asarray(column_waves(g)), both, nc, size)


def solution(mesh):
    placed = (
        P(("group", "wide"), None, None),
        P(("group", "wide"), None, None),
        P(("group", "wide")),
        P(("group", "wide")),
        P(("group", "wide")),
        P(("group", "wide")),
    )
    return jax.shard_map(
        per_device, mesh=mesh, in_specs=placed, out_specs=P(None, "group", "wide"), check_vma=False
    )
```

```python
import functools
import math

import jax
import jax.numpy as jnp
import numpy as np
from jax import lax
from jax.experimental import pallas as pl
from jax.experimental.pallas import tpu as pltpu
from jax.sharding import PartitionSpec as P

SUB = 32
HALF = SUB // 2
VIS = 128
GRID = 4096
TILES = GRID // SUB
F32 = jnp.float32
BF16 = jnp.bfloat16


def _poly_coefs(most, degree):
    top = most**2
    nodes = top / 2 * (1 + np.cos(np.pi * (np.arange(64) + 0.5) / 64))
    r = np.sqrt(nodes)
    cheb = np.polynomial.chebyshev.Chebyshev
    c = cheb.fit(nodes, np.cos(2 * np.pi * r), degree, domain=[0, top])
    s = cheb.fit(nodes, np.sin(2 * np.pi * r) / r, degree, domain=[0, top])
    poly = np.polynomial.Polynomial
    return (
        [float(v) for v in c.convert(kind=poly).coef],
        [float(v) for v in s.convert(kind=poly).coef],
    )


ANY_TURN = _poly_coefs(0.5, 5)
SMALL_TURN = _poly_coefs((SUB / 2 - 2) / (2 * SUB), 4)


def cis(r, coefs):
    z = r * r
    c, s = coefs[0][-1], coefs[1][-1]
    for k in range(len(coefs[0]) - 2, -1, -1):
        c = c * z + coefs[0][k]
        s = s * z + coefs[1][k]
    return c, s * r


def cmul(a, b):
    return a[0] * b[0] - a[1] * b[1], a[0] * b[1] + a[1] * b[0]


def split(x):
    hi = x.astype(BF16)
    lo = (x - hi.astype(F32)).astype(BF16)
    return hi, lo


def np_tables():
    t = np.arange(SUB)
    q = np.arange(SUB)
    n0 = np.arange(TILES)
    g = np.einsum(
        "tq,qn->tn",
        np.exp(-2j * np.pi * np.outer(t, q) / SUB),
        np.exp(-2j * np.pi * np.outer(q, n0) / GRID),
    )
    w = np.exp(-2j * np.pi * (np.outer(n0, n0) % TILES) / TILES)
    return g, w


def to_waves(g):
    sign = (-1.0) ** np.arange(HALF)[None, :, None]
    up = g[:, HALF:] * sign
    down = g[:, HALF - 1 :: -1] * -sign
    return np.concatenate([up + down, 1j * (up - down)], 1)


def shifted(g):
    index = (np.arange(SUB)[:, None] + np.arange(SUB)[None, :]) % SUB
    return to_waves(g[index])


def pixel_rows(raw_ref, size, out_ref, row_ref, wave_ref, send):
    lane = lax.broadcasted_iota(jnp.int32, (SUB, VIS), 1)
    step = (lax.broadcasted_iota(jnp.int32, (8, VIS), 0).astype(F32) + 0.5) / SUB
    cat = jnp.concatenate

    def prepare(t):
        ar, ai, u, v = (raw_ref[q * size + t * 8 : q * size + t * 8 + 8] for q in range(4))
        first_u, first_v = (cis((x - HALF) * (1.0 / (2 * SUB)), SMALL_TURN) for x in (u, v))
        twice = cmul(first_u, first_u)
        wave = first_u
        for m in range(8):
            if m:
                wave = cmul(wave, twice)
            for part in range(2):
                row = t * 8 * 16 + part * 8 + m
                wave_ref[pl.ds(row, 8, stride=16), :] = wave[part]
        step_u = cmul(wave, first_u)
        step_v = first_v
        for _ in range(4):
            step_v = cmul(step_v, step_v)
        pr, pi = cmul(first_u, first_v)
        rows = [*step_u, *step_v, ar * pr + ai * pi, ai * pr - ar * pi, v - HALF]
        for q, row in enumerate(rows):
            row_ref[t, q] = row

    def parts(n):
        t, d = n // 8, n % 8
        bc = lambda q: jnp.broadcast_to(row_ref[t, q, d : d + 1, :], (8, VIS))
        ur, ui, vr, vi, ar, ai, v = (bc(q) for q in range(7))
        cu, su = (wave_ref[n * 16 + q * 8 : n * 16 + q * 8 + 8] for q in range(2))
        turns = v * step
        cv, sv = cis(turns - jnp.round(turns), ANY_TURN)
        ahead = lambda c, s, r, i: [c, c * r - s * i, s, c * i + s * r]
        us = ahead(cu, su, ur, ui)
        vs = ahead(cv, sv, vr, vi)
        wh, wl = split(cat([ar * x for x in us] + [ai * x for x in us], 0))
        vh, vl = split(cat(vs, 0))
        return cat([wh, wl], 1), cat([vh, vh], 1), cat([vl, vl], 1)

    def pair(n):
        one, two = parts(n), parts(n + 1)
        prod = lax.dot_general(
            cat([one[0], two[0]], 0),
            cat([one[1], two[1], one[2], two[2]], 0),
            (((1,), (1,)), ((), ())),
            preferred_element_type=F32,
        )
        ar, ai, br, bi = (prod[q * SUB : q * SUB + SUB] for q in range(4))
        fold = lambda p, q, r, s: jnp.where(
            lane < 64, jnp.where(lane < 32, p, q), jnp.where(lane < 96, r, s)
        )
        out_ref[n // 2] = fold(ar, bi, ai, br) + pltpu.roll(fold(ai, br, ar, bi), 64, 1)

    prepare(0)
    for t in range(size // 8):
        if t + 1 < size // 8:
            prepare(t + 1)
        for d in range(0, 8, 2):
            pair(t * 8 + d)
        if (t + 1) * 16 % size == 0:
            send((t + 1) * 16 // size - 1)


def gather_kernel(
    wide, subs, size, band, count_ref, owner_ref, row_in_ref, col_ref, vis_ref, off_ref,
    pix_hbm, ids_hbm,
    raw_ref, row_ref, wave_ref, out_ref,
    send_sem, recv_sem, loc_sem, pix_send, pix_recv, id_loc, id_send, id_recv,
):
    depth = wide // 4
    pieces = subs // size
    trips = 2 * depth * pieces
    relays = (depth - 1) * pieces
    me = lax.axis_index("wide")
    core, y, z = me % 2, (me // 2) % 2, me // 4
    place = lambda zz, yy, cc: (zz * 2 + yy) * 2 + cc
    partner = {"wide": place(z, y, 1 - core)}
    across = {"wide": place(z, 1 - y, core)}
    above = {"wide": place(jnp.minimum(z + 1, depth - 1), y, core)}
    below = {"wide": place(jnp.maximum(z - 1, 0), y, core)}
    not_top, not_bottom = z < depth - 1, z > 0
    mesh_id = pl.DeviceIdType.MESH
    here = z * 2 + y

    barrier = pltpu.get_barrier_semaphore()
    for peer in (partner, across):
        pl.semaphore_signal(barrier, inc=1, device_id=peer, device_id_type=mesh_id)

    @pl.when(not_top)
    def _():
        pl.semaphore_signal(barrier, inc=1, device_id=above, device_id_type=mesh_id)

    @pl.when(not_bottom)
    def _():
        pl.semaphore_signal(barrier, inc=1, device_id=below, device_id_type=mesh_id)

    slots = lax.broadcasted_iota(jnp.int32, (8, VIS), 1)
    def stage_piece(piece):
        def stage(t, ids):
            for d in range(8):
                j = t * 8 + d
                n = piece * size + j
                live = jnp.where(slots[:2] < count_ref[n], 1.0 / math.sqrt(VIS), 0.0)
                for half, pair in enumerate((vis_ref[n] * live, off_ref[n])):
                    for q in range(2):
                        raw_ref[here, piece, pl.ds((half * 2 + q) * size + j, 1), :] = pair[q : q + 1]
                tile = (owner_ref[n] * band + row_in_ref[n]) * TILES + col_ref[n]
                ids = jnp.where(slots == j, tile, ids)
            return ids

        ids = lax.fori_loop(0, size // 8, stage, jnp.zeros((8, VIS), jnp.int32))
        raw_ref[here, piece, 4 * size :, :] = ids.astype(F32)

    stage_piece(0)
    neighbours = jnp.minimum(z, 1) + jnp.minimum(depth - 1 - z, 1)
    pl.semaphore_wait(barrier, 2 + neighbours)

    def hop(zz, yy, piece, to, way):
        chip = zz * 2 + yy
        return pltpu.make_async_remote_copy(
            src_ref=raw_ref.at[chip, piece],
            dst_ref=raw_ref.at[chip, piece],
            send_sem=send_sem.at[zz, piece, way],
            recv_sem=recv_sem.at[chip, piece],
            device_id=to,
            device_id_type=mesh_id,
        )

    def spread_out(zz, piece, act):
        act(hop(zz, y, piece, across, 2))

        @pl.when((zz <= z) & not_top)
        def _():
            act(hop(zz, y, piece, above, 0))

        @pl.when((zz >= z) & not_bottom)
        def _():
            act(hop(zz, y, piece, below, 1))

    spread_out(z, 0, lambda copy: copy.start())
    for piece in range(1, pieces):
        stage_piece(piece)

    def pass_on(number):
        far, piece = number // pieces + 1, number % pieces
        for zz, inside in ((z - far, z - far >= 0), (z + far, z + far < depth)):

            @pl.when(inside)
            def _():
                hop(zz, y, piece, across, 2).wait_recv()
                spread_out(zz, piece, lambda copy: copy.start())

    near = jnp.minimum(z, depth - 1 - z)

    def order(k):
        swing = z + ((k + 1) // 2) * (1 - 2 * (k % 2))
        edge = jnp.where(z * 2 < depth - 1, k, depth - 1 - k)
        return jnp.where(k <= 2 * near, swing, edge)

    def copies(number, chip, piece, half):
        part = size // 4
        rows = pl.ds(((chip * 2 + core) * subs + piece * size) // 2 + half * part, part)
        slot = number % 2 * 2 + half
        block = out_ref.at[number % 2, pl.ds(half * part, part)]
        mine = pltpu.make_async_copy(block, pix_hbm.at[rows], loc_sem.at[slot])
        theirs = pltpu.make_async_remote_copy(
            src_ref=block,
            dst_ref=pix_hbm.at[rows],
            send_sem=pix_send.at[slot],
            recv_sem=pix_recv.at[number * 2 + half],
            device_id=partner,
            device_id_type=mesh_id,
        )
        return mine, theirs

    def id_copies(number, chip, piece):
        block = raw_ref.at[chip, piece, pl.ds(4 * size, 8)]
        where = ids_hbm.at[(chip * 2 + core) * pieces + piece]
        mine = pltpu.make_async_copy(block, where, id_loc.at[number])
        theirs = pltpu.make_async_remote_copy(
            src_ref=block,
            dst_ref=where,
            send_sem=id_send.at[number],
            recv_sem=id_recv.at[number],
            device_id=partner,
            device_id_type=mesh_id,
        )
        return mine, theirs

    def body(number, carry):
        later = number - pieces
        end = later - 2 * relays
        other = jnp.where(later >= 0, jnp.where(end >= 0, 1, 1 - later % 2), 0)
        at_turn = jnp.where(later >= 0, jnp.where(end >= 0, relays + end, later // 2), number)
        relayed = jnp.where(later >= 0, 1 - other, 0)
        relay = at_turn - pieces * (1 - relayed)
        first = relay < 0
        paired = relay < 2 * near * pieces
        group = 2 * pieces
        k = jnp.where(paired, 1 + relay // group * 2 + relay % 2, 1 + relay // pieces)
        k = jnp.where(first, 0, k)
        piece = jnp.where(paired, relay % group // 2, relay % pieces)
        piece = jnp.where(first, at_turn, piece)
        zz = order(k)
        yy = y + other * (1 - 2 * y)
        chip = zz * 2 + yy

        @pl.when(other == 1)
        def _():
            hop(zz, yy, piece, across, 2).wait_recv()

        for copy in id_copies(number, chip, piece):
            copy.start()

        @pl.when(number >= 2)
        def _():
            for half in range(2):
                mine, theirs = copies(number, chip, piece, half)
                mine.wait()
                theirs.wait_send()

        def send(half):
            for copy in copies(number, chip, piece, half):
                copy.start()

        pixel_rows(raw_ref.at[chip, piece], size, out_ref.at[number % 2], row_ref, wave_ref, send)

        @pl.when(number + 1 < pieces)
        def _():
            spread_out(z, number + 1, lambda copy: copy.start())

        @pl.when((number % 2 == 1) & (number // 2 < relays))
        def _():
            pass_on(number // 2)

        return carry

    lax.fori_loop(0, trips, body, 0)

    def drain(number, carry):
        spread_out(number // pieces, number % pieces, lambda copy: copy.wait_send())
        return carry

    lax.fori_loop(0, depth * pieces, drain, 0)
    for number in range(2):
        for half in range(2):
            mine, theirs = copies(number, here, 0, half)
            mine.wait()
            theirs.wait_send()

    def arrive(number, carry):
        mine, theirs = id_copies(number, here, 0)
        mine.wait()
        theirs.wait()
        for half in range(2):
            copies(number, here, 0, half)[1].wait_recv()
        return carry

    lax.fori_loop(0, trips, arrive, 0)


def gather(scalars, visibilities, offsets, wide, size, band):
    subs = visibilities.shape[0]
    depth = wide // 4
    pieces = subs // size
    trips = 2 * depth * pieces
    dma = pltpu.SemaphoreType.DMA
    anywhere = pl.BlockSpec(memory_space=pl.ANY)
    whole = pl.BlockSpec(memory_space=pltpu.VMEM)
    return pl.pallas_call(
        functools.partial(gather_kernel, wide, subs, size, band),
        out_shape=[
            jax.ShapeDtypeStruct((wide * subs // 2, SUB, 128), F32),
            jax.ShapeDtypeStruct((wide * pieces, 8, 128), F32),
        ],
        in_specs=[pl.BlockSpec(memory_space=pltpu.SMEM)] * 4 + [whole, whole],
        out_specs=[anywhere, anywhere],
        scratch_shapes=[
            pltpu.VMEM((wide // 2, pieces, 4 * size + 8, 128), F32),
            pltpu.VMEM((size // 8, 7, 8, VIS), F32),
            pltpu.VMEM((size * 16, VIS), F32),
            pltpu.VMEM((2, size // 2, SUB, 128), F32),
            dma((depth, pieces, 3)),
            dma((wide // 2, pieces)),
            dma((4,)),
            dma((4,)),
            dma((2 * trips,)),
            dma((trips,)),
            dma((trips,)),
            dma((trips,)),
        ],
        compiler_params=pltpu.CompilerParams(collective_id=0, has_side_effects=True),
        name="gather",
    )(*scalars, visibilities, offsets)


def fft(xs):
    n = len(xs)
    if n == 1:
        return xs
    even, odd = fft(xs[::2]), fft(xs[1::2])
    low, high = [], []
    root = math.sqrt(0.5)
    for k, ((er, ei), (r, i)) in enumerate(zip(even, odd)):
        if k == 0:
            tr, ti = r, i
        elif 4 * k == n:
            low.append((er + i, ei - r))
            high.append((er - i, ei + r))
            continue
        elif 8 * k == n:
            tr, ti = (r + i) * root, (i - r) * root
        elif 8 * k == 3 * n:
            tr, ti = (i - r) * root, (r + i) * -root
        else:
            tr, ti = turn(r, i, k / n)
        low.append((er + tr, ei + ti))
        high.append((er - tr, ei - ti))
    return low + high


def turn(r, i, turns):
    c, s = math.cos(2 * math.pi * turns), math.sin(2 * math.pi * turns)
    return r * c + i * s, i * c - r * s


def finish_kernel(
    block, size, nc, shift, p_ref, ids_ref, phr_ref, phi_ref, waves_hbm, mix_hbm, out_hbm,
    x_ref, b_ref, y_ref, tab_ref, wave_ref, mix_ref, idv_ref, ids_smem, sem, id_sem, mix_sem, out_sem,
):
    g = pl.program_id(0)
    steps = pl.num_programs(0)
    halves = nc // 128
    chunk = 16
    rows = chunk * 16

    @pl.when(g == 0)
    def _():
        first = lax.axis_index("wide") * halves
        pltpu.make_async_copy(mix_hbm, mix_ref, mix_sem).start()
        load = pltpu.make_async_copy(waves_hbm.at[pl.ds(first, halves)], wave_ref, sem)
        load.start()

        def number(t, carry):
            idv_ref[pl.ds(t, 1), :] = ids_ref[t, 0:1, :].astype(jnp.int32)
            return carry

        lax.fori_loop(0, ids_ref.shape[0], number, 0, unroll=4)
        scalars = pltpu.make_async_copy(idv_ref, ids_smem, id_sem)
        scalars.start()

        def zero(t, carry):
            for lt in range(2 * halves):
                for ref in (b_ref, x_ref):
                    ref[lt, pl.ds(t * 32, 32), :] = jnp.zeros((32, 128), F32)
            return carry

        lax.fori_loop(0, TILES, zero, 0)
        load.wait()
        tab_ref[...] = jnp.zeros(tab_ref.shape, BF16)
        for n in range(halves):
            left = slice(n * 128, n * 128 + 128)
            right = slice(nc + n * 128, nc + n * 128 + 128)
            for row, low in ((0, 0), (32, 0), (128, 64)):
                dr = wave_ref[n, low : low + 32]
                di = wave_ref[n, low + 32 : low + 64]
                tab_ref[row : row + 32, left] = dr
                tab_ref[row : row + 32, right] = di
                tab_ref[row + 64 : row + 96, left] = -di
                tab_ref[row + 64 : row + 96, right] = dr
        scalars.wait()

    early = lax.broadcasted_iota(jnp.int32, (rows, 128), 1) % 64 < 32

    def multiply(t, slot):
        p = p_ref[pl.ds(t * chunk // 2, chunk // 2)].reshape(rows, 128)
        hi = p.astype(BF16)
        hif = hi.astype(F32)
        lof = p - hif
        lo = lof.astype(BF16)
        hir = pltpu.roll(hi, 32, 1)
        one = jnp.where(early, hi, pltpu.roll(lo, 32, 1))
        two = jnp.where(early, hir, pltpu.roll(lo, 64, 1))
        lhs = jnp.concatenate(
            [
                jnp.concatenate([one, hi], 1),
                jnp.concatenate([two, hir], 1),
            ],
            0,
        )
        y_ref[slot] = jnp.dot(lhs, tab_ref[...], preferred_element_type=F32)

    def add(t, slot):
        for d in range(chunk):
            at = t * chunk + d
            tile = ids_smem[g * (block // size) + at // size, at % size]
            r = lax.shift_right_logical(tile, shift)
            c = lax.bitwise_and(tile, TILES - 1)
            pr = jnp.broadcast_to(phr_ref[pl.ds(c, 1), :], (8, 128))
            pi = jnp.broadcast_to(phi_ref[pl.ds(c, 1), :], (8, 128))
            dst = pl.ds(pl.multiple_of(r * 32, 32), 32)
            acc = b_ref if d % 2 else x_ref
            old = acc[:, dst, :]
            y = y_ref[slot, pl.ds(d % 2 * rows + d // 2 * SUB, SUB), :]
            real, imag = [], []
            for n in range(halves):
                yr = y[:, n * 128 : n * 128 + 128].reshape(4, 8, 128)
                yi = y[:, nc + n * 128 : nc + n * 128 + 128].reshape(4, 8, 128)
                real.append((yr * pr - yi * pi).reshape(1, 32, 128))
                imag.append((yr * pi + yi * pr).reshape(1, 32, 128))
            acc[:, dst, :] = old + jnp.concatenate(real + imag, 0)

    trips = block // chunk
    multiply(0, 0)
    for t in range(trips):
        if t + 1 < trips:
            multiply(t + 1, (t + 1) % 2)
        add(t, t % 2)

    @pl.when(g == steps - 1)
    def _():
        at = lambda r, it: pl.ds(pl.multiple_of(r * 32 + it * 8, 8), 8)

        def eights(t, carry):
            n, it = t // 4, t % 4
            for b in range(16):
                xs = []
                for a in range(8):
                    pick = at(16 * a + b, it)
                    xs.append(
                        tuple(
                            x_ref[o * halves + n, pick, :] + b_ref[o * halves + n, pick, :]
                            for o in range(2)
                        )
                    )
                for k, (r, i) in enumerate(fft(xs)):
                    if b * k:
                        r, i = turn(r, i, b * k / TILES)
                    pick = at(16 * k + b, it)
                    x_ref[n, pick, :] = r
                    x_ref[halves + n, pick, :] = i
            return carry

        def sixteens(t, carry):
            n, it = t // 4, t % 4
            for a in range(8):
                xs = []
                for b in range(16):
                    pick = at(16 * a + b, it)
                    xs.append((x_ref[n, pick, :], x_ref[halves + n, pick, :]))
                for k, (r, i) in enumerate(fft(xs)):
                    pick = at(a + 8 * k, it)
                    b_ref[n, pick, :] = r
                    b_ref[halves + n, pick, :] = i
            return carry

        def mix(t, carry):
            parts = []
            for d in range(8):
                m = t * 8 + d
                near = pl.ds(pl.multiple_of(m * SUB, SUB), SUB)
                zm = jnp.concatenate(
                    [
                        jnp.concatenate([b_ref[o * halves + n, near, :] for n in range(halves)], 1)
                        for o in range(2)
                    ],
                    0,
                )
                zh, zl = split(zm)
                both = mix_ref[m]
                res = jnp.dot(
                    jnp.concatenate([both, both[:, :64]], 1),
                    jnp.concatenate([zh, zh, zl], 0),
                    preferred_element_type=F32,
                )
                parts.append(res[None])
            for n in range(halves):
                for q in range(8):
                    block8 = jnp.concatenate(
                        [p[:, q * 8 : q * 8 + 8, n * 128 : n * 128 + 128] for p in parts], 0
                    )
                    turned = jnp.transpose(block8, (1, 0, 2))
                    for e in range(8):
                        p, b = divmod(q * 8 + e, SUB)
                        far = pl.ds(pl.multiple_of(b * TILES + t * 8, 8), 8)
                        x_ref[p * halves + n, far, :] = turned[e]
            rows8 = pl.ds(pl.multiple_of(t * 8, 8), 8)
            for p in range(2):
                for n in range(halves):
                    pltpu.make_async_copy(
                        x_ref.reshape(2 * halves, SUB, TILES, 128).at[p * halves + n, :, rows8],
                        out_hbm.reshape(2, SUB, TILES, nc).at[p, :, rows8, pl.ds(n * 128, 128)],
                        out_sem.at[p * halves + n],
                    ).start()
            return carry

        lax.fori_loop(0, 4 * halves, eights, 0)
        lax.fori_loop(0, 4 * halves, sixteens, 0)
        pltpu.make_async_copy(mix_hbm, mix_ref, mix_sem).wait()
        lax.fori_loop(0, TILES // 8, mix, 0)
        for p in range(2):
            for n in range(halves):
                pltpu.make_async_copy(
                    x_ref.at[p * halves + n],
                    out_hbm.at[p, :, pl.ds(n * 128, 128)],
                    out_sem.at[p * halves + n],
                ).wait()


def finish(pix, ids, phr, phi, waves, mix, nc, size):
    count = pix.shape[0] * 2
    block = math.gcd(count, 2 * size)
    tiles = 2 * nc // 128
    const = lambda shape: pl.BlockSpec(shape, lambda g: (0,) * len(shape))
    anywhere = pl.BlockSpec(memory_space=pl.ANY)
    x_shape = (tiles, GRID, 128)
    dma = pltpu.SemaphoreType.DMA
    return pl.pallas_call(
        functools.partial(finish_kernel, block, size, nc, TILES.bit_length() - 1),
        out_shape=jax.ShapeDtypeStruct((2, GRID, nc), F32),
        grid=(count // block,),
        in_specs=[
            pl.BlockSpec((block // 2, SUB, 128), lambda g: (g, 0, 0)),
            const(ids.shape),
            const(phr.shape),
            const(phi.shape),
            anywhere,
            anywhere,
        ],
        out_specs=anywhere,
        scratch_shapes=[
            pltpu.VMEM(x_shape, F32),
            pltpu.VMEM(x_shape, F32),
            pltpu.VMEM((2, 512, 2 * nc), F32),
            pltpu.VMEM((256, 2 * nc), BF16),
            pltpu.VMEM((nc // 128, 128, 128), BF16),
            pltpu.VMEM(mix.shape, BF16),
            pltpu.VMEM((count // size, 128), jnp.int32),
            pltpu.SMEM((count // size, 128), jnp.int32),
            dma,
            dma,
            dma,
            dma((tiles,)),
        ],
        name="finish",
    )(pix, ids, phr, phi, waves, mix)


def np_split(x):
    hi = x.astype(np.float32).astype(BF16)
    return hi, (x - hi.astype(np.float64)).astype(BF16)


def column_waves(g):
    waves = shifted(g) / 512.0
    rh, rl = np_split(waves.real)
    ih, il = np_split(waves.imag)
    return np.concatenate([rh, ih, rl, il], 1)


def real_form(z):
    return np.array([[z.real, -z.imag], [z.imag, z.real]])


def per_device(visibilities, offsets, vis_count, owner, tile_row, tile_col):
    wide = lax.axis_size("wide")
    nc = GRID // wide
    band = GRID // (SUB * wide)
    g, w = np_tables()
    subs = visibilities.shape[0]
    size = math.gcd(subs, 96)
    scalars = (vis_count, owner, tile_row, tile_col)
    pix, ids = gather(scalars, visibilities, offsets, wide, size, band)
    m4 = real_form(shifted(g) / 256.0).transpose(4, 0, 2, 1, 3).reshape(TILES, 64, 64)
    both = jnp.asarray(np.concatenate(np_split(m4), 2))
    phr, phi = jnp.asarray(w.real, F32), jnp.asarray(w.imag, F32)
    return finish(pix, ids, phr, phi, jnp.asarray(column_waves(g)), both, nc, size)


def solution(mesh):
    placed = (
        P(("group", "wide"), None, None),
        P(("group", "wide"), None, None),
        P(("group", "wide")),
        P(("group", "wide")),
        P(("group", "wide")),
        P(("group", "wide")),
    )
    return jax.shard_map(
        per_device, mesh=mesh, in_specs=placed, out_specs=P(None, "group", "wide"), check_vma=False
    )
```
